32 devices in a mesh: batch: 8 (over z, x), row: 2 (over y), col: 2 (over core).
Axes of the slice: x: 2, y: 2, z: 4, core: 2. Of those that a mesh axis runs over, the one named last changes fastest.
Arguments:
- basis_values: bfloat16 [32, 192, 2048], P(('batch', 'row', 'col')), may hold values from -6 to 6
- density_matrix: bfloat16 [32, 3, 192, 192], P(('batch', 'row', 'col')), may hold values from -0.03125 to 0.03125
- points: float32 [32, 3, 2048], P(('batch', 'row', 'col')), may hold values from -2 to 2
- weights: float32 [32, 2048], P(('batch', 'row', 'col')), may hold values from 0.128 to 1.28
- intersection: int32 [32, 32], P(('batch', 'row', 'col')), may hold values from 0 to 31, as said below
- basis_index: int32 [32, 192], P(('batch', 'row', 'col')), may hold values from 0 to 1535, as said below
- atom_positions: float32 [3, 32], replicated, may hold values from -2 to 2
- shell_blocks: int32 [32], replicated, may hold values from 1 to 8
- shell_widths: float32 [64], replicated, may hold values from 0.03125 to 0.0625
- green: bfloat16 [32, 8, 4096], P('batch'), may hold values from -0.0009765625 to 0.0009765625
Outputs:
- potential: bfloat16 [32, 12288], P('batch')
- hamiltonian: bfloat16 [3, 1536, 1536], P(None, 'row', 'col')
The draws below stay inside these ranges and needn't reach their ends.
Inputs may be any that keep to these rules, and one draw needn't show every extreme that they name: `intersection`: within a batch the 32 atom numbers are distinct. The owner of atom a is a // 4; no owner holds more than 4 of one batch's atoms, and among the batches with equal row and col index one owner holds exactly 4 of the atoms of every such batch. `basis_index`: within a batch the numbers are distinct, and its q-th run of 96 entries lies in [q * 768, (q + 1) * 768).
All inputs are finite; a program needn't handle non-finite values.
Results may differ from the reference program's by a relative error of at most 0.0095.
Values may be sent and summed in bfloat16 or wider, within the bound.
No kernel may reach another device: no remote copies, remote signals or barrier semaphores. Data moves between devices by JAX's collectives and lax.ppermute only.
A program may use at most 128 MiB of HBM per device.

```python
import math
import jax
import jax.numpy as jnp
from jax import lax

NBF = 192
P_SIZE = 2048
S = 64
DEG = 8
K_OV = 32
A_DEV = 4
NB = 1536
L = 64
SHB = 8
BATCHES = 32
ATOMS = 32
N_BATCH = 8
N_ROW = 2
N_COL = 2


def draw_intersection(key, part):
    batches = N_BATCH * N_ROW * N_COL
    planes = N_ROW * N_COL
    cap = (K_OV + N_BATCH - 1) // N_BATCH
    pairs = N_BATCH * cap
    base = jax.random.fold_in(key, 11)
    first_key, second_key, third_key = jax.random.split(base, 3)
    star = jax.random.randint(first_key, (planes,), 0, N_BATCH)
    plane_of = jnp.arange(batches) % planes
    star_of = jnp.take(star, plane_of)
    noise = jax.random.randint(second_key, (batches, pairs), 0, 1 << 20)
    pair_ids = jnp.arange(pairs)
    special = pair_ids[None, :] // cap == star_of[:, None]
    score = (noise + jnp.where(special, 1 << 21, 0)) * pairs + pair_ids[None, :]
    chosen = lax.top_k(score, K_OV)[1]
    owner = chosen // cap
    rank = chosen % cap
    orders = jax.vmap(lambda single: jax.random.permutation(single, A_DEV))(jax.random.split(third_key, batches))
    local = jnp.take_along_axis(orders, rank, axis=1)
    return (owner * A_DEV + local).astype(jnp.int32)


def draw_basis_index(key, part):
    batches = N_BATCH * N_ROW * N_COL
    span = NB // N_ROW
    each = NBF // N_ROW
    keys = jax.random.split(jax.random.fold_in(key, 23), batches * N_ROW)
    picks = jax.vmap(lambda single: jax.random.permutation(single, span)[:each])(keys).reshape(batches, N_ROW, each)
    offsets = (jnp.arange(N_ROW) * span)[None, :, None]
    return (picks + offsets).reshape(batches, NBF).astype(jnp.int32)


def place_ends(values, rng, low, high):
    index_at = [jax.random.randint(jax.random.fold_in(rng, axis), (), 0, length) for axis, length in enumerate(values.shape)]
    widest = values.shape.index(max(values.shape))
    neighbour = index_at[:widest] + [(index_at[widest] + 1) % values.shape[widest]] + index_at[widest + 1:]
    return values.at[tuple(index_at)].set(low).at[tuple(neighbour)].set(high)


def level_of(key, extent, cuts, low, largest):
    def one(position, shards_of):
        draws = jax.random.uniform(jax.random.fold_in(jax.random.fold_in(key, 6), position), (shards_of,), jnp.float32, low / len(cuts), largest / len(cuts))
        return jnp.repeat(jnp.exp(draws), extent[position] // shards_of).reshape((-1,) + (1,) * (len(extent) - position - 1))

    gain = one(*cuts[0])
    for cut in cuts[1:]:
        gain = gain * one(*cut)
    return gain


def centred(key, shape, scale, limit, pieces=(), held_as=jnp.bfloat16):
    array = scale * jax.random.normal(key, shape, jnp.float32)
    if pieces:
        array = array * level_of(key, shape, pieces, -0.22, 0.18)
    return jnp.clip(array, -limit, limit).astype(held_as)


def setup_inputs(seed: int = 0) -> dict:
    seeds = jax.random.split(jax.random.key(seed), 11)
    basis_values = centred(seeds[0], (BATCHES, NBF, P_SIZE), 1.0, 6.0, ((0, 32),))
    density_matrix = centred(seeds[1], (BATCHES, 3, NBF, NBF), (1.0 / NBF), 0.03125, ((0, 32),))
    points = jnp.clip(jax.random.uniform(seeds[2], (BATCHES, 3, P_SIZE), jnp.float32, -2.0, 2.0) * level_of(seeds[2], (BATCHES, 3, P_SIZE), ((0, 32),), -0.4, 0.0), -2.0, 2.0)
    weights = jnp.clip(jnp.exp(math.log(1.28) - 2.30258502 * jax.random.uniform(seeds[3], (BATCHES, P_SIZE), jnp.float32) ** level_of(seeds[3], (BATCHES, P_SIZE), ((0, 32),), -0.2, 0.2)), 0.128, 1.28)
    intersection = draw_intersection(jax.random.fold_in(seeds[10], 71), 0)
    basis_index = draw_basis_index(jax.random.fold_in(seeds[10], 71), 0)
    atom_positions = jnp.clip(jax.random.uniform(seeds[6], (3, ATOMS), jnp.float32, -2.0, 2.0), -2.0, 2.0)
    shell_blocks = place_ends(jax.random.randint(seeds[7], (ATOMS,), 1, SHB + 1), jax.random.fold_in(seeds[7], 1), 1, SHB).astype(jnp.int32)
    shell_widths = jnp.clip(jnp.exp(jax.random.uniform(seeds[8], (S,), jnp.float32, math.log(0.03125), math.log(0.0625))), 0.03125, 0.0625)
    green = centred(seeds[9], (ATOMS, DEG, S * S), (4 * S * L * L * K_OV) ** -0.5, 0.0009765625, ((0, 8),))
    return dict(basis_values=basis_values, density_matrix=density_matrix, points=points, weights=weights, intersection=intersection, basis_index=basis_index, atom_positions=atom_positions, shell_blocks=shell_blocks, shell_widths=shell_widths, green=green)


def chebyshev(values, count):
    terms = [jnp.ones_like(values), values]
    for order in range(2, count):
        terms.append(2.0 * values * terms[-1] - terms[-2])
    return jnp.stack(terms[:count], axis=0)

def atom_tables(spots, centre, blocks, shell_widths):
    delta = spots - centre[:, None]
    dist = jnp.sqrt(lax.optimization_barrier(jnp.sum(delta * delta, axis=0)) + 0.01)
    unit = delta / dist[None, :]
    shells = shell_widths.shape[0]
    middle = 4.0 * jnp.arange(shells).astype(jnp.float32) / shells
    live = jnp.arange(shells).astype(jnp.int32) < 8 * blocks
    bump = jnp.exp(-jnp.square((dist[None, :] - middle[:, None]) / shell_widths[:, None]))
    radial = jnp.where(live[:, None], bump, jnp.zeros_like(bump))
    polar = chebyshev(unit[2], DEG)
    side = chebyshev(unit[0], DEG)
    angular = (polar[:, None, :] * side[None, :, :]).reshape(DEG * DEG, spots.shape[1])
    return (radial, angular.astype(jnp.bfloat16))

def batch_tables(spots, atoms, atom_positions, shell_blocks, shell_widths):
    centres = jnp.take(atom_positions, atoms, axis=1).T
    counts = jnp.take(shell_blocks, atoms)
    return jax.vmap(atom_tables, in_axes=(None, 0, 0, None))(spots, centres, counts, shell_widths)

def reference(basis_values, density_matrix, points, weights, intersection, basis_index, atom_positions, shell_blocks, shell_widths, green):
    atoms_total = green.shape[0]
    width = 3 * S * DEG * DEG
    highest = lax.Precision.HIGHEST

    def first_pass(total, item):
        phi, dens, spots, measure, atoms = item
        phi_wide = phi.astype(jnp.float32)
        dphi = jnp.einsum('cij,jp->cip', dens.astype(jnp.float32), phi_wide)
        density = lax.optimization_barrier(jnp.sum(phi_wide[None] * dphi, axis=1))
        radial, angular = batch_tables(spots, atoms, atom_positions, shell_blocks, shell_widths)
        weighted = measure[None, :] * density
        scaled = lax.optimization_barrier((radial[:, None] * weighted[None, :, None, :]).astype(jnp.bfloat16))
        moments = jnp.einsum('kcsp,klp->kcsl', scaled.astype(jnp.float32), angular.astype(jnp.float32))
        return (total.at[atoms].add(moments.reshape(atoms.shape[0], width)), None)
    total, _ = lax.scan(first_pass, jnp.zeros((atoms_total, width), jnp.float32), (basis_values, density_matrix, points, weights, intersection))
    charges = lax.optimization_barrier(total.astype(jnp.bfloat16)).astype(jnp.float32)
    charges = charges.reshape(atoms_total, 3, S, DEG, DEG)
    kernels = green.astype(jnp.float32).reshape(atoms_total, DEG, S, S)
    potential = jnp.einsum('xast,xctam->xcsam', kernels, charges).astype(jnp.bfloat16).reshape(atoms_total, width)

    def second_pass(tiles, item):
        phi, spots, measure, atoms, labels = item
        radial, angular = batch_tables(spots, atoms, atom_positions, shell_blocks, shell_widths)
        tables = jnp.take(potential, atoms, axis=0).astype(jnp.float32).reshape(atoms.shape[0], 3, S, DEG * DEG)
        spread = jnp.einsum('kcsl,klp->kcsp', tables, angular.astype(jnp.float32))
        field = jnp.einsum('ksp,kcsp->cp', radial, spread, precision=highest)
        phi_wide = phi.astype(jnp.float32)
        operand = lax.optimization_barrier((phi_wide[None] * (measure[None, :] * field)[:, None, :]).astype(jnp.bfloat16))
        local = jnp.einsum('cip,jp->cij', operand.astype(jnp.float32), phi_wide)
        local = lax.optimization_barrier(local.astype(jnp.bfloat16)).astype(jnp.float32)
        return (tiles.at[:, labels[:, None], labels[None, :]].add(local), None)
    tiles, _ = lax.scan(second_pass, jnp.zeros((3, NB, NB), jnp.float32), (basis_values, points, weights, intersection, basis_index))
    return (potential, tiles.astype(jnp.bfloat16))
```

```python
import jax
import jax.numpy as jnp
from jax import lax
from jax.sharding import PartitionSpec as P

S = 64
DEG = 8
NB = 1536


def chebyshev(values, count):
    terms = [jnp.ones_like(values), values]
    for order in range(2, count):
        terms.append(2.0 * values * terms[-1] - terms[-2])
    return jnp.stack(terms[:count], axis=0)


def atom_tables(spots, centre, blocks, shell_widths):
    delta = spots - centre[:, None]
    dist = jnp.sqrt(jnp.sum(delta * delta, axis=0) + 0.01)
    unit = delta / dist[None, :]
    shells = shell_widths.shape[0]
    middle = 4.0 * jnp.arange(shells).astype(jnp.float32) / shells
    live = jnp.arange(shells) < 8 * blocks
    bump = jnp.exp(-jnp.square((dist[None, :] - middle[:, None]) / shell_widths[:, None]))
    radial = jnp.where(live[:, None], bump, jnp.zeros_like(bump))
    polar = chebyshev(unit[2], DEG)
    side = chebyshev(unit[0], DEG)
    angular = (polar[:, None, :] * side[None, :, :]).reshape(DEG * DEG, spots.shape[1])
    return (radial, angular.astype(jnp.bfloat16))


def apply_green(charges, kernels):
    shaped = charges.astype(jnp.bfloat16).reshape(-1, 3, S, DEG, DEG)
    kernel_rows = kernels.reshape(-1, DEG, S, S)
    result = jnp.einsum(
        "xast,xctam->xcsam", kernel_rows, shaped, preferred_element_type=jnp.float32
    )
    return result.astype(jnp.bfloat16).reshape(-1, 3 * S * DEG * DEG)


def swap(value, axis, mask):
    size = lax.axis_size(axis)
    return lax.ppermute(value, axis, [(i, i ^ mask) for i in range(size)])


def owner_steps():
    owners = lax.axis_size("batch")
    high = 1 << (owners.bit_length() - 1)
    masks = [1]
    bit = high >> 1
    while bit > 1:
        masks.append(bit)
        bit >>= 1
    steps = [("col", 1), ("row", 1)]
    return steps + [("batch", mask) for mask in masks[: owners.bit_length() - 1]]


def relative_atoms(steps):
    cols, rows = lax.axis_size("col"), lax.axis_size("row")
    mine = {
        "col": lax.axis_index("col"),
        "row": lax.axis_index("row"),
        "batch": lax.axis_index("batch"),
    }
    total = 1 << len(steps)
    flip = {"col": [], "row": [], "batch": []}
    for place in range(total):
        masks = {"col": 0, "row": 0, "batch": 0}
        for order, (axis, mask) in enumerate(steps):
            if (place >> (len(steps) - 1 - order)) & 1:
                masks[axis] |= mask
        for axis in flip:
            flip[axis].append(masks[axis])
    there = {axis: jnp.array(flip[axis], jnp.int32) ^ mine[axis] for axis in flip}
    return (there["batch"] * rows + there["row"]) * cols + there["col"]


def sum_to_owner(moments, steps):
    held = moments
    for axis, mask in steps:
        half = held.shape[0] // 2
        got = swap(held[half:].astype(jnp.bfloat16), axis, mask)
        held = held[:half] + got.astype(jnp.float32)
    return held


def gather_from_owners(value, steps):
    held = value
    for axis, mask in reversed(steps):
        held = jnp.concatenate([held, swap(held, axis, mask)], axis=0)
    return held


def place_quads(stack, reach, tile):
    count, parts, piece = stack.shape[0], 3, reach
    body = parts * piece * piece // 128
    blocks = stack[:, :body].reshape(count, parts, piece, piece)
    tail = stack[:, body:].reshape(count, -1).astype(jnp.int32)
    labels = tail[:, : 2 * piece] * 32 + tail[:, 2 * piece : 4 * piece]
    grid = jnp.arange(tile)
    rows_hit = (grid[:, None] == labels[:, :piece].reshape(-1)[None, :]).astype(jnp.bfloat16)
    cols_hit = (labels[:, piece:, None] == grid[None, None, :]).astype(jnp.bfloat16)
    wide = jnp.einsum(
        "gcij,gju->cgiu", blocks, cols_hit, preferred_element_type=jnp.float32
    ).astype(jnp.bfloat16)
    return jnp.einsum(
        "tk,cku->ctu",
        rows_hit,
        wide.reshape(parts, count * piece, tile),
        preferred_element_type=jnp.float32,
    )


def on_device(
    basis_values,
    density_matrix,
    points,
    weights,
    intersection,
    basis_index,
    atom_positions,
    shell_blocks,
    shell_widths,
    green,
):
    phi = basis_values[0]
    dens = density_matrix[0]
    spots = points[0]
    measure = weights[0]
    atoms = intersection[0]
    labels = basis_index[0]
    owners = lax.axis_size("batch")
    parts = lax.axis_size("row")
    sides = lax.axis_size("col")
    row, col = lax.axis_index("row"), lax.axis_index("col")
    count = atoms.shape[0]
    slots = (count + owners - 1) // owners
    holding = green.shape[0]
    every_atom = atom_positions.shape[1]
    width = 3 * S * DEG * DEG
    highest = lax.Precision.HIGHEST
    dense = (
        count == every_atom
        and parts == 2
        and sides == 2
        and holding == parts * sides
        and owners & (owners - 1) == 0
    )
    steps = owner_steps() if dense else None
    if dense:
        atoms = relative_atoms(steps)
    dphi = jnp.einsum("cij,jp->cip", dens, phi, preferred_element_type=jnp.float32)
    phi_wide = phi.astype(jnp.float32)
    density = jnp.sum(phi_wide[None] * dphi, axis=1)
    weighted = measure[None, :] * density
    picked = jnp.arange(every_atom)[:, None] == atoms[None, :]
    centres = jnp.dot(atom_positions, picked.astype(jnp.float32), precision=highest)
    blocks = jnp.sum(jnp.where(picked, shell_blocks[:, None], 0), axis=0)
    group = min(8, count)
    starts = list(range(0, count, group))
    make_tables = jax.vmap(atom_tables, in_axes=(None, 1, 0, None))
    kept = []
    pieces = []
    for first in starts:
        radial, angular = make_tables(
            spots, centres[:, first : first + group], blocks[first : first + group], shell_widths
        )
        kept.append((radial, angular))
        scaled = (radial[:, None] * weighted[None, :, None, :]).astype(jnp.bfloat16)
        pieces.append(
            jnp.einsum("kcsp,klp->kcsl", scaled, angular, preferred_element_type=jnp.float32)
        )
    moments = jnp.concatenate(pieces, axis=0).reshape(count, width)
    if dense:
        packed = moments.reshape(count, width // 128, 128)
        charges = sum_to_owner(packed, steps)
        kernels = lax.dynamic_index_in_dim(green, row * sides + col, 0, keepdims=True)
        mine = apply_green(charges.reshape(1, width), kernels).reshape(1, width // 128, 128)
        tables = gather_from_owners(mine, steps)
        plane = tables.reshape(2, 2, owners, width)[:, :, 0]
        plane = jnp.where(row == 0, plane, plane[:, ::-1])
        plane = jnp.where(col == 0, plane, plane[::-1])
        potential = jnp.swapaxes(plane, 0, 1).reshape(holding, width)
    else:
        home = atoms // holding
        local_slot = atoms % holding
        order = jnp.arange(count)
        before = (home[None, :] == home[:, None]) & (order[None, :] < order[:, None])
        place = home * slots + jnp.sum(before, axis=1)
        routing = jnp.arange(owners * slots)[:, None] == place[None, :]
        outgoing = jnp.dot(routing.astype(jnp.float32), moments, precision=highest).reshape(
            owners, slots, width
        )
        tags = (jnp.sum(jnp.where(routing, local_slot[None, :] + 1, 0), axis=1) - 1).reshape(
            owners, slots
        )
        incoming, sources = (
            lax.all_to_all(outgoing, "batch", split_axis=0, concat_axis=0, tiled=True),
            lax.all_to_all(tags, "batch", split_axis=0, concat_axis=0, tiled=True),
        )
        collect = jnp.arange(holding)[:, None] == sources.reshape(1, owners * slots)
        partial_value = jnp.dot(
            collect.astype(jnp.float32), incoming.reshape(owners * slots, width), precision=highest
        )
        totals = lax.psum(partial_value, ("row", "col"))
        potential = apply_green(totals, green)
        back = jnp.dot(
            collect.T.astype(jnp.bfloat16), potential, preferred_element_type=jnp.float32
        ).astype(jnp.bfloat16)
        returned = lax.all_to_all(
            back.reshape(owners, slots, width), "batch", split_axis=0, concat_axis=0, tiled=True
        )
        tables = jnp.dot(
            routing.T.astype(jnp.bfloat16),
            returned.reshape(owners * slots, width),
            preferred_element_type=jnp.float32,
        )
    tables = tables.astype(jnp.bfloat16).reshape(count, 3, S, DEG * DEG)
    field = jnp.zeros((3, spots.shape[1]), jnp.float32)
    for position, first in enumerate(starts):
        radial, angular = kept[position]
        spread = jnp.einsum(
            "kcsl,klp->kcsp",
            tables[first : first + group],
            angular,
            preferred_element_type=jnp.float32,
        )
        field = field + jnp.einsum("ksp,kcsp->cp", radial, spread, precision=highest)
    piece = labels.shape[0] // parts
    operand = (phi_wide[None] * (measure[None, :] * field)[:, None, :]).astype(jnp.bfloat16)
    quads = jnp.einsum(
        "cxip,yjp->yxcij",
        operand.reshape(3, parts, piece, -1),
        phi.reshape(sides, piece, -1),
        preferred_element_type=jnp.float32,
    ).astype(jnp.bfloat16)
    tile = NB // parts
    inner = labels.reshape(parts, piece) - jnp.arange(parts)[:, None] * tile
    digits = jnp.stack([inner // 32, inner % 32], axis=0).astype(jnp.bfloat16)
    by_row = jnp.broadcast_to(digits[:, None, :, :], (2, sides, parts, piece))
    by_col = jnp.broadcast_to(digits[:, :, None, :], (2, sides, parts, piece))
    tail = jnp.stack([by_row, by_col], axis=3)
    tail = jnp.moveaxis(tail, 0, 2).reshape(sides, parts, 4 * piece)
    extra = -(4 * piece) % 128
    tail = jnp.pad(tail, ((0, 0), (0, 0), (0, extra))).reshape(sides, parts, -1, 128)
    load = jnp.concatenate([quads.reshape(sides, parts, -1, 128), tail], axis=2)
    pad_rows = -load.shape[2] % 16
    load = jnp.pad(load, ((0, 0), (0, 0), (0, pad_rows), (0, 0)))
    keep = lax.dynamic_index_in_dim(load, col, 0, keepdims=False)
    give = lax.dynamic_index_in_dim(load, 1 - col, 0, keepdims=False)
    pair = jnp.stack([keep, swap(give, "col", 1)], axis=1)
    keep = lax.dynamic_index_in_dim(pair, row, 0, keepdims=False)
    give = lax.dynamic_index_in_dim(pair, 1 - row, 0, keepdims=False)
    plane_load = jnp.concatenate([keep, swap(give, "row", 1)], axis=0)
    if owners <= 8:
        lines = [plane_load] + [swap(plane_load, "batch", m) for m in range(2, owners, 2)]
        stack = jnp.concatenate(lines + [swap(line, "batch", 1) for line in lines], axis=0)
        total = place_quads(stack, piece, tile)
    else:
        everyone = lax.all_gather(plane_load, "batch", axis=0)

        def add(total, item):
            return total + place_quads(item.reshape((-1,) + item.shape[2:]), piece, tile), None

        chunk = 8
        everyone = everyone.reshape((owners // chunk, chunk) + plane_load.shape)
        total, _ = lax.scan(add, jnp.zeros((3, tile, tile), jnp.float32), everyone)
    return (potential, total.astype(jnp.bfloat16))


def solution(mesh):
    return jax.shard_map(
        on_device,
        mesh=mesh,
        in_specs=(
            P(("batch", "row", "col"), None, None),
            P(("batch", "row", "col"), None, None, None),
            P(("batch", "row", "col"), None, None),
            P(("batch", "row", "col"), None),
            P(("batch", "row", "col"), None),
            P(("batch", "row", "col"), None),
            P(),
            P(),
            P(),
            P("batch", None, None),
        ),
        out_specs=(P("batch", None), P(None, "row", "col")),
        check_vma=False,
    )
```

```python
import functools

import jax
import jax.numpy as jnp
from jax import lax
from jax.experimental import pallas as pl
from jax.experimental.pallas import tpu as pltpu
from jax.sharding import PartitionSpec as P

S = 64
DEG = 8
NB = 1536
LANES = 128
FAR = 1.0e6
LOG2E = 1.4426950408889634
NT = (((1,), (1,)), ((), ()))
SMEM = pl.BlockSpec(memory_space=pltpu.SMEM)
VMEM = pl.BlockSpec(memory_space=pltpu.VMEM)


def prepare(first, count, atoms_ref, pos_ref, pts_ref, dist_ref, polar_ref, side_ref):
    rows = lax.broadcasted_iota(jnp.int32, (count, LANES), 0)
    centre = []
    for axis in range(3):
        column = jnp.zeros((count, LANES), jnp.float32)
        for k in range(count):
            column = jnp.where(rows == k, pos_ref[axis, atoms_ref[first + k]], column)
        centre.append(column)
    for start in range(0, pts_ref.shape[1], LANES):
        here = pl.ds(start, LANES)
        delta = [pts_ref[pl.ds(axis, 1), here] - centre[axis] for axis in range(3)]
        square = delta[0] * delta[0] + delta[1] * delta[1] + delta[2] * delta[2] + 0.01
        inverse = lax.rsqrt(square)
        dist_ref[start // LANES] = square * inverse
        for ladder, u in ((polar_ref, delta[2] * inverse), (side_ref, delta[0] * inverse)):
            older, old = jnp.ones_like(u), u
            ladder[start // LANES, pl.ds(0, count), :] = older
            ladder[start // LANES, pl.ds(count, count), :] = old
            for order in range(2, DEG):
                older, old = old, 2.0 * u * old - older
                ladder[start // LANES, pl.ds(order * count, count), :] = old


def shell_columns(blocks, widths_ref):
    place = lax.broadcasted_iota(jnp.int32, (S, LANES), 0)
    shell = jnp.where(place < S // 2, 2 * place, 2 * place - (S - 1))
    middle = jnp.where(shell < 8 * blocks, shell.astype(jnp.float32) * (4.0 / S), FAR)
    return middle


def angular_tile(k, count, t, polar_ref, side_ref):
    side = side_ref[t, pl.ds(k, DEG, stride=count), :]
    return jnp.concatenate(
        [polar_ref[t, pl.ds(order * count + k, DEG, stride=0), :] * side for order in range(DEG)], axis=0
    ).astype(jnp.bfloat16)


def radial_tile(k, t, middle, scale, dist_ref):
    gap = jnp.concatenate([dist_ref[t, pl.ds(k, 8, stride=0), :]] * (S // 8), axis=0) - middle
    return jnp.exp2(gap * (gap * scale))


def moments_kernel(first, count, chunk, fresh, *refs):
    if fresh:
        (atoms_ref, pos_ref, blocks_ref, pts_ref, scale_ref, phi_ref, dens_ref, w_ref,
         out_ref, wd_ref, dist_ref, polar_ref, side_ref) = refs
    else:
        (atoms_ref, pos_ref, blocks_ref, pts_ref, scale_ref, wd_ref,
         out_ref, dist_ref, polar_ref, side_ref) = refs
    points = pts_ref.shape[1]
    if fresh:
        for start in range(0, points, 256):
            here = pl.ds(start, 256)
            phi = phi_ref[:, here]
            wide = phi.astype(jnp.float32)
            for c in range(3):
                product = jnp.dot(dens_ref[c], phi, preferred_element_type=jnp.float32)
                wd_ref[pl.ds(c, 1), here] = w_ref[:, here] * jnp.sum(
                    wide * product, axis=0, keepdims=True)
    prepare(first, count, atoms_ref, pos_ref, pts_ref, dist_ref, polar_ref, side_ref)

    def body(k, carry):
        middle = shell_columns(blocks_ref[atoms_ref[first + k]], None)
        scale = scale_ref[...]
        total = jnp.zeros((3 * S, S), jnp.float32)
        for start in range(0, points, chunk):
            scaled, angles = [[], [], []], []
            for inner in range(start, start + chunk, LANES):
                here = pl.ds(inner, LANES)
                radial = radial_tile(k, here.start // LANES, middle, scale, dist_ref)
                angles.append(angular_tile(k, count, here.start // LANES, polar_ref, side_ref))
                for c in range(3):
                    scaled[c].append((radial * wd_ref[pl.ds(c, 1), here]).astype(jnp.bfloat16))
            left = jnp.concatenate([jnp.concatenate(s, axis=1) for s in scaled], axis=0)
            right = jnp.concatenate(angles, axis=1)
            total += lax.dot_general(left, right, NT, preferred_element_type=jnp.float32)
        for c in range(3):
            even, odd = total[c * S : c * S + S // 2], total[c * S + S // 2 : (c + 1) * S]
            out_ref[k, pl.ds(c * (S // 2), S // 2), :] = jnp.concatenate(
                [even, odd], axis=1).astype(out_ref.dtype)
        return carry

    lax.fori_loop(0, count, body, 0)


def moments_call(first, count, atoms, pos, blocks, pts, scale, wd=None, phi=None, dens=None, w=None, chunk=256):
    points = pts.shape[1]
    fresh = wd is None
    out = [jax.ShapeDtypeStruct((count, 3 * S // 2, LANES), jnp.bfloat16)]
    args = [atoms, pos, blocks, pts, scale]
    if fresh:
        out.append(jax.ShapeDtypeStruct((3, points), jnp.float32))
        args += [phi, dens, w]
    else:
        args += [wd]
    scratch = [pltpu.VMEM((points // LANES, count, LANES), jnp.float32)] + [pltpu.VMEM((points // LANES, DEG * count, LANES), jnp.float32)] * 2
    cost = count * points
    return pl.pallas_call(
        functools.partial(moments_kernel, first, count, chunk, fresh),
        out_shape=out,
        in_specs=[SMEM] * 3 + [VMEM] * (len(args) - 3),
        out_specs=[VMEM] * len(out),
        scratch_shapes=scratch,
        cost_estimate=pl.CostEstimate(flops=cost * 3 * S * S * 2, bytes_accessed=cost * 8, transcendentals=cost * S),
        name="moments",
    )(*args)


def field_kernel(first, count, last, *refs):
    if last:
        (atoms_ref, pos_ref, blocks_ref, pts_ref, scale_ref, tab_ref, acc_in, phi_ref, w_ref, marks_ref, flip_ref,
         out_ref, dist_ref, polar_ref, side_ref, acc_ref, oper_ref) = refs
    else:
        (atoms_ref, pos_ref, blocks_ref, pts_ref, scale_ref, tab_ref, acc_in,
         acc_ref, dist_ref, polar_ref, side_ref) = refs
    points = pts_ref.shape[1]
    prepare(first, count, atoms_ref, pos_ref, pts_ref, dist_ref, polar_ref, side_ref)
    acc_ref[...] = acc_in[...]

    def body(k, carry):
        middle = shell_columns(blocks_ref[atoms_ref[first + k]], None)
        scale = scale_ref[...]
        table = tab_ref[k]
        halves = (table[:, : S], table[:, S:])
        for start in range(0, points, 256):
            right = jnp.concatenate(
                [angular_tile(k, count, (start + d) // LANES, polar_ref, side_ref) for d in (0, LANES)], axis=1)
            spread = [jnp.dot(h, right, preferred_element_type=jnp.float32) for h in halves]
            for d in (0, LANES):
                here = pl.ds(start + d, LANES)
                radial = radial_tile(k, here.start // LANES, middle, scale, dist_ref)
                for c in range(3):
                    sums = acc_ref[pl.ds(8 * c, 8), here]
                    for h in range(2):
                        for r in range(0, S // 2, 8):
                            sums += (radial[h * (S // 2) + r : h * (S // 2) + r + 8]
                                     * spread[h][c * (S // 2) + r : c * (S // 2) + r + 8, d : d + LANES])
                    acc_ref[pl.ds(8 * c, 8), here] = sums
        return carry

    lax.fori_loop(0, count, body, 0)
    if last:
        piece = phi_ref.shape[0] // 2
        quads = {}
        for c in range(3):
            for start in range(0, points, 256):
                here = pl.ds(start, 256)
                scale_row = w_ref[:, here] * jnp.sum(acc_ref[pl.ds(8 * c, 8), here], axis=0, keepdims=True)
                oper_ref[:, here] = (phi_ref[:, here].astype(jnp.float32) * scale_row).astype(jnp.bfloat16)
            for x in range(2):
                for y in range(2):
                    quads[c, x, y] = lax.dot_general(
                        oper_ref[pl.ds(x * piece, piece), :], phi_ref[pl.ds(y * piece, piece), :], NT,
                        preferred_element_type=jnp.float32)
        for x in range(2):
            for y in range(2):
                q0, q1, q2 = (quads[c, x, y] for c in range(3))
                third = piece // 3
                there = (y ^ flip_ref[0], x ^ flip_ref[1])
                marks = jnp.concatenate(
                    [marks_ref[x], marks_ref[y], jnp.zeros((third - 16, third), jnp.float32)], axis=0)
                parts = [q2[b * third : (b + 1) * third, 2 * third :] for b in range(3)] + [marks]
                blocks = [
                    jnp.concatenate([q0, q2[:, :third]], axis=1),
                    jnp.concatenate([q1, q2[:, third : 2 * third]], axis=1),
                    jnp.concatenate(parts, axis=1),
                ]
                out_ref[there[0], there[1]] = jnp.concatenate(blocks, axis=0).astype(jnp.bfloat16)


def field_call(first, count, atoms, pos, blocks, pts, scale, tables, acc, phi=None, w=None, marks=None, flip=None):
    points = pts.shape[1]
    last = phi is not None
    args = [atoms, pos, blocks, pts, scale, tables, acc]
    scratch = [pltpu.VMEM((points // LANES, count, LANES), jnp.float32)] + [pltpu.VMEM((points // LANES, DEG * count, LANES), jnp.float32)] * 2
    if last:
        args += [phi, w, marks, flip]
        third = phi.shape[0] // 6
        out = jax.ShapeDtypeStruct((2, 2, 7 * third, LANES), jnp.bfloat16)
        scratch += [pltpu.VMEM((24, points), jnp.float32), pltpu.VMEM(phi.shape, jnp.bfloat16)]
    else:
        out = jax.ShapeDtypeStruct((24, points), jnp.float32)
    cost = count * points
    return pl.pallas_call(
        functools.partial(field_kernel, first, count, last),
        out_shape=out,
        in_specs=[SMEM] * 3 + [VMEM] * (len(args) - 3 - last) + [SMEM] * last,
        out_specs=VMEM,
        scratch_shapes=scratch,
        cost_estimate=pl.CostEstimate(flops=cost * 3 * S * S * 2, bytes_accessed=cost * 8, transcendentals=cost * S),
        name="field",
    )(*args)


def place_kernel(pieces, carried, final, piece, tile, *refs):
    stacks, refs = refs[:pieces], refs[pieces:]
    if carried:
        acc_in, refs = refs[0], refs[1:]
    out_ref, rows_ref, wide_ref = refs
    third = piece // 3
    group = 4
    total = rows_ref.shape[1] // piece
    lane = lax.broadcasted_iota(jnp.int32, (piece, LANES), 1)
    sub = lax.broadcasted_iota(jnp.int32, (tile, LANES), 0)
    per = total // pieces
    for first in range(0, total, group):
        strips = []
        for g in range(first, first + group):
            ref, at = stacks[g // per], g % per
            tail = ref[at, pl.ds(2 * piece, third), :].astype(jnp.float32)
            marks = tail[: third // 2, 3 * third :]
            row_mark = marks[0:3] * 32.0 + marks[3:6]
            col_mark = marks[8:11] * 32.0 + marks[11:14]
            strips += [row_mark[b : b + 1] for b in range(3)]
            flat = jnp.concatenate([col_mark[b : b + 1] for b in range(3)] + [col_mark[0:1]], axis=1)
            column = jnp.transpose(jnp.broadcast_to(flat, (LANES, LANES)))[:piece].astype(jnp.int32)
            hits = jnp.concatenate(
                [(column == lane + u).astype(jnp.float32).astype(jnp.bfloat16) for u in range(0, tile, LANES)], axis=1)
            upper = ref[at, pl.ds(0, piece), :].astype(jnp.float32)
            lower = ref[at, pl.ds(piece, piece), :].astype(jnp.float32)
            rest = jnp.concatenate([tail[:, b * third : (b + 1) * third] for b in range(3)], axis=0)
            third_part = jnp.concatenate([upper[:, piece:], lower[:, piece:], rest], axis=1)
            quads = jnp.concatenate([upper[:, :piece], lower[:, :piece], third_part], axis=0).astype(jnp.bfloat16)
            spread = jnp.dot(quads, hits, preferred_element_type=jnp.float32).astype(jnp.bfloat16)
            for c in range(3):
                wide_ref[c, pl.ds(g * piece, piece), :] = spread[c * piece : (c + 1) * piece]
        strip = jnp.concatenate(strips, axis=1).astype(jnp.int32)
        for start in range(0, group * piece, LANES):
            rows_ref[:, pl.ds(first * piece + start, LANES)] = (
                sub == strip[:, start : start + LANES]).astype(jnp.float32).astype(jnp.bfloat16)

    step = 256
    def body(i, carry):
        c, t = i // (tile // step), (i % (tile // step)) * step
        here = pl.ds(pl.multiple_of(t, step), step)
        value = jnp.dot(rows_ref[here, :], wide_ref[c], preferred_element_type=jnp.float32)
        if carried:
            value += acc_in[c, here, :]
        out_ref[c, here, :] = value.astype(out_ref.dtype)
        return carry
    lax.fori_loop(0, 3 * (tile // step), body, 0)

def place_call(stacks, piece, tile, acc=None, final=True):
    total = sum(s.shape[0] for s in stacks)
    depth = total * piece
    args = list(stacks) + ([acc] if acc is not None else [])
    return pl.pallas_call(
        functools.partial(place_kernel, len(stacks), acc is not None, final, piece, tile),
        out_shape=jax.ShapeDtypeStruct((3, tile, tile), jnp.bfloat16 if final else jnp.float32),
        in_specs=[VMEM] * len(args), out_specs=VMEM,
        scratch_shapes=[pltpu.VMEM((tile, depth), jnp.bfloat16), pltpu.VMEM((3, depth, tile), jnp.bfloat16)],
        compiler_params=pltpu.CompilerParams(vmem_limit_bytes=60 << 20),
        cost_estimate=pl.CostEstimate(flops=2 * 3 * depth * tile * tile, bytes_accessed=12 * tile * tile, transcendentals=0),
        name="place",
    )(*args)


def apply_green(charges, kernels):
    shaped = charges.astype(jnp.bfloat16).reshape(-1, 3, S, DEG, DEG)
    kernel_rows = kernels.reshape(-1, DEG, S, S)
    result = jnp.einsum(
        "xast,xctam->xcsam", kernel_rows, shaped, preferred_element_type=jnp.float32
    )
    return result.astype(jnp.bfloat16).reshape(-1, 3 * S * DEG * DEG)


def swap(value, axis, mask=1):
    size = lax.axis_size(axis)
    return lax.ppermute(value, axis, [(i, i ^ mask) for i in range(size)])


def plane_atoms(owners, row, col):
    flips = jnp.arange(4)
    inner = ((flips & 1) ^ row) * 2 + ((flips >> 1) ^ col)
    return (jnp.arange(owners)[None, :] * 4 + inner[:, None]).reshape(-1)


def on_device(
    basis_values,
    density_matrix,
    points,
    weights,
    intersection,
    basis_index,
    atom_positions,
    shell_blocks,
    shell_widths,
    green,
):
    phi = basis_values[0]
    dens = density_matrix[0]
    spots = points[0]
    atoms = intersection[0]
    labels = basis_index[0]
    owners = lax.axis_size("batch")
    parts = lax.axis_size("row")
    sides = lax.axis_size("col")
    row, col = lax.axis_index("row"), lax.axis_index("col")
    count = atoms.shape[0]
    slots = (count + owners - 1) // owners
    holding = green.shape[0]
    every_atom = atom_positions.shape[1]
    width = 3 * S * DEG * DEG
    lines = width // LANES
    highest = lax.Precision.HIGHEST
    dense = count == every_atom and holding == parts * sides
    if dense:
        atoms = plane_atoms(owners, row, col)
    group = count // 4
    ordered = jnp.concatenate([shell_widths[0::2], shell_widths[1::2]])
    scale = jnp.broadcast_to((-LOG2E / (ordered * ordered))[:, None], (S, LANES))
    shared = (atoms, atom_positions, shell_blocks, spots, scale)

    def moments_of(place, weighted):
        return moments_call(place * group, group, *shared, wd=weighted)[0]

    third, weighted = moments_call(
        3 * group, group, *shared, phi=phi, dens=dens, w=weights
    )
    if dense:
        from_third = swap(third, "col")
        first = moments_of(1, weighted) + from_third
        from_first = swap(first, "row")
        from_second = swap(moments_of(2, weighted), "col")
        held = (
            moments_of(0, weighted).astype(jnp.float32)
            + from_second.astype(jnp.float32)
            + from_first.astype(jnp.float32)
        ).astype(jnp.bfloat16)
        shares = lax.all_to_all(held, "batch", split_axis=0, concat_axis=0, tiled=True)
        charges = jnp.sum(shares.astype(jnp.float32), axis=0)
        kernels = lax.dynamic_index_in_dim(green, row * sides + col, 0, keepdims=True)
        mine = apply_green(charges.reshape(1, width), kernels).reshape(1, lines, LANES)
        own = lax.all_to_all(
            jnp.broadcast_to(mine, (owners, lines, LANES)),
            "batch",
            split_axis=0,
            concat_axis=0,
            tiled=True,
        )
        beside = swap(own, "row")
        tables = [own, beside, swap(own, "col"), swap(beside, "col")]
        here = lax.axis_index("batch")
        plane = jnp.stack(
            [lax.dynamic_index_in_dim(table, here, 0, keepdims=False) for table in tables]
        )
        places = [(j // sides ^ row) + 2 * (j % sides ^ col) for j in range(holding)]
        potential = jnp.concatenate(
            [lax.dynamic_index_in_dim(plane, place, 0) for place in places]
        ).reshape(holding, width)
    else:
        moments = jnp.concatenate([moments_of(place, weighted) for place in range(3)] + [third])
        moments = moments.astype(jnp.float32).reshape(count, width)
        home = atoms // holding
        local_slot = atoms % holding
        order = jnp.arange(count)
        before = (home[None, :] == home[:, None]) & (order[None, :] < order[:, None])
        place = home * slots + jnp.sum(before, axis=1)
        routing = jnp.arange(owners * slots)[:, None] == place[None, :]
        outgoing = jnp.dot(routing.astype(jnp.float32), moments, precision=highest).reshape(
            owners, slots, width
        )
        tags = (jnp.sum(jnp.where(routing, local_slot[None, :] + 1, 0), axis=1) - 1).reshape(
            owners, slots
        )
        incoming, sources = (
            lax.all_to_all(outgoing, "batch", split_axis=0, concat_axis=0, tiled=True),
            lax.all_to_all(tags, "batch", split_axis=0, concat_axis=0, tiled=True),
        )
        collect = jnp.arange(holding)[:, None] == sources.reshape(1, owners * slots)
        partial_value = jnp.dot(
            collect.astype(jnp.float32), incoming.reshape(owners * slots, width), precision=highest
        )
        totals = lax.psum(partial_value, ("row", "col"))
        potential = apply_green(totals, green)
        back = jnp.dot(
            collect.T.astype(jnp.bfloat16), potential, preferred_element_type=jnp.float32
        ).astype(jnp.bfloat16)
        returned = lax.all_to_all(
            back.reshape(owners, slots, width), "batch", split_axis=0, concat_axis=0, tiled=True
        )
        table = jnp.dot(
            routing.T.astype(jnp.bfloat16),
            returned.reshape(owners * slots, width),
            preferred_element_type=jnp.float32,
        )
        table = table.astype(jnp.bfloat16).reshape(count, lines, LANES)
        tables = [table[place * group : (place + 1) * group] for place in range(4)]
    piece = labels.shape[0] // parts
    tile = NB // parts
    inner = labels.reshape(parts, 3, piece // 3) - jnp.arange(parts)[:, None, None] * tile
    marks = jnp.concatenate([inner // 32, inner % 32, inner[:, :2] * 0], axis=1)
    marks = marks.astype(jnp.float32)
    field = jnp.zeros((24, spots.shape[1]), jnp.float32)
    for place in (0, 2, 1):
        field = field_call(place * group, group, *shared, tables[place], field)
    flip = jnp.stack([col, row])
    load = field_call(
        3 * group, group, *shared, tables[3], field, phi=phi, w=weights, marks=marks, flip=flip
    )
    fresh = swap(load[1], "col")
    got = swap(jnp.stack([load[0, 1], fresh[1]]), "row")
    plane_load = jnp.concatenate([load[0, :1], fresh[:1], got], axis=0)
    if owners <= 8:
        near = [plane_load] + [swap(plane_load, "batch", m) for m in range(2, owners, 2)]
        far = [swap(line, "batch") for line in near]
        total = place_call(near, piece, tile, final=False)
        hamiltonian = place_call(far, piece, tile, acc=total)
    else:
        everyone = lax.all_gather(plane_load, "batch", axis=0)
        chunk = 4
        everyone = everyone.reshape((owners // chunk, chunk * 4) + plane_load.shape[1:])

        def add(total, item):
            return place_call([item], piece, tile, acc=total, final=False), None

        total, _ = lax.scan(add, jnp.zeros((3, tile, tile), jnp.float32), everyone)
        hamiltonian = total.astype(jnp.bfloat16)
    return (potential, hamiltonian)


def solution(mesh):
    return jax.shard_map(
        on_device,
        mesh=mesh,
        in_specs=(
            P(("batch", "row", "col"), None, None),
            P(("batch", "row", "col"), None, None, None),
            P(("batch", "row", "col"), None, None),
            P(("batch", "row", "col"), None),
            P(("batch", "row", "col"), None),
            P(("batch", "row", "col"), None),
            P(),
            P(),
            P(),
            P("batch", None, None),
        ),
        out_specs=(P("batch", None), P(None, "row", "col")),
        check_vma=False,
    )
```

```python
import functools

import jax
import jax.numpy as jnp
from jax import lax
from jax.experimental import pallas as pl
from jax.experimental.pallas import tpu as pltpu
from jax.sharding import PartitionSpec as P

S = 64
DEG = 8
NB = 1536
LANES = 128
FAR = 1.0e6
LOG2E = 1.4426950408889634
NT = (((1,), (1,)), ((), ()))
SMEM = pl.BlockSpec(memory_space=pltpu.SMEM)
VMEM = pl.BlockSpec(memory_space=pltpu.VMEM)


def prepare(first, count, atoms_ref, pos_ref, pts_ref, dist_ref, polar_ref, side_ref):
    rows = lax.broadcasted_iota(jnp.int32, (count, LANES), 0)
    centre = []
    for axis in range(3):
        column = jnp.zeros((count, LANES), jnp.float32)
        for k in range(count):
            column = jnp.where(rows == k, pos_ref[axis, atoms_ref[first + k]], column)
        centre.append(column)
    for t in range(pts_ref.shape[2] // LANES):
        here = pl.ds(t * LANES, LANES)
        delta = [pts_ref[0, pl.ds(axis, 1), here] - centre[axis] for axis in range(3)]
        square = delta[0] * delta[0] + delta[1] * delta[1] + delta[2] * delta[2] + 0.01
        inverse = lax.rsqrt(square)
        dist_ref[t] = square * inverse
        for ladder, u in ((polar_ref, delta[2] * inverse), (side_ref, delta[0] * inverse)):
            older, old = jnp.ones_like(u), u
            ladder[t, pl.ds(0, count), :] = older
            ladder[t, pl.ds(count, count), :] = old
            for order in range(2, DEG):
                older, old = old, 2.0 * u * old - older
                ladder[t, pl.ds(order * count, count), :] = old


def prepare_shells(widths_ref, scale_ref):
    rows = lax.broadcasted_iota(jnp.int32, (8, LANES), 0)
    for start in range(0, S, 8):
        column = jnp.zeros((8, LANES), jnp.float32)
        for j in range(8):
            place = start + j
            shell = 2 * place if place < S // 2 else 2 * place - (S - 1)
            column = jnp.where(rows == j, widths_ref[shell], column)
        scale_ref[pl.ds(start, 8), :] = -LOG2E / (column * column)


def shell_columns(blocks, live, scale_ref):
    half = live // 2
    place = lax.broadcasted_iota(jnp.int32, (live, LANES), 0)
    shell = jnp.where(place < half, 2 * place, 2 * place - (live - 1))
    middle = jnp.where(shell < 8 * blocks, shell.astype(jnp.float32) * (4.0 / S), FAR)
    scale = jnp.concatenate(
        [scale_ref[pl.ds(0, half), :], scale_ref[pl.ds(S // 2, half), :]], axis=0
    )
    return middle, scale


def angular_tile(k, count, t, polar_ref, side_ref):
    side = side_ref[t, pl.ds(k, DEG, stride=count), :]
    return jnp.concatenate(
        [
            polar_ref[t, pl.ds(order * count + k, DEG, stride=0), :] * side
            for order in range(DEG)
        ],
        axis=0,
    ).astype(jnp.bfloat16)


def radial_tile(k, t, middle, scale, dist_ref):
    dist = dist_ref[t, pl.ds(k, 8, stride=0), :]
    gap = jnp.concatenate([dist] * (middle.shape[0] // 8), axis=0) - middle
    return jnp.exp2(gap * (gap * scale))


def by_live(blocks, run):
    for live in range(16, S + 1, 16):

        @pl.when((blocks * 8 > live - 16) & (blocks * 8 <= live))
        def _(live=live):
            run(live)


def moments_kernel(first, count, fresh, *refs):
    if fresh:
        (
            atoms_ref, pos_ref, blocks_ref, widths_ref, pts_ref, phi_ref, dens_ref, w_ref,
            out_ref, wd_ref, dist_ref, polar_ref, side_ref, scale_ref,
        ) = refs
    else:
        (
            atoms_ref, pos_ref, blocks_ref, widths_ref, pts_ref, wd_ref,
            out_ref, dist_ref, polar_ref, side_ref, scale_ref,
        ) = refs
    points = pts_ref.shape[2]
    if fresh:
        for start in range(0, points, 256):
            here = pl.ds(start, 256)
            phi = phi_ref[0, :, here]
            wide = phi.astype(jnp.float32)
            for c in range(3):
                product = jnp.dot(dens_ref[0, c], phi, preferred_element_type=jnp.float32)
                density = jnp.sum(wide * product, axis=0, keepdims=True)
                wd_ref[pl.ds(c, 1), here] = w_ref[:, here] * density
    prepare(first, count, atoms_ref, pos_ref, pts_ref, dist_ref, polar_ref, side_ref)
    prepare_shells(widths_ref, scale_ref)

    def body(k, carry):
        blocks = blocks_ref[atoms_ref[first + k]]

        def run(live):
            middle, scale = shell_columns(blocks, live, scale_ref)
            total = jnp.zeros((3 * live, S), jnp.float32)
            for start in range(0, points, 256):
                scaled, angles = [[], [], []], []
                for inner in (start, start + LANES):
                    t = inner // LANES
                    radial = radial_tile(k, t, middle, scale, dist_ref).astype(jnp.bfloat16)
                    angles.append(angular_tile(k, count, t, polar_ref, side_ref))
                    for c in range(3):
                        row = jnp.broadcast_to(wd_ref[pl.ds(c, 1), pl.ds(inner, LANES)], (16, LANES))
                        row = jnp.concatenate([row.astype(jnp.bfloat16)] * (live // 16), axis=0)
                        scaled[c].append(radial * row)
                left = jnp.concatenate([jnp.concatenate(s, axis=1) for s in scaled], axis=0)
                right = jnp.concatenate(angles, axis=1)
                total += lax.dot_general(left, right, NT, preferred_element_type=jnp.float32)
            half = live // 2
            for c in range(3):
                even = total[c * live : c * live + half]
                odd = total[c * live + half : (c + 1) * live]
                block = jnp.concatenate([even, odd], axis=1)
                if live < S:
                    rest = jnp.zeros((S // 2 - half, LANES), jnp.float32)
                    block = jnp.concatenate([block, rest], axis=0)
                out_ref[k, pl.ds(c * (S // 2), S // 2), :] = block.astype(out_ref.dtype)

        by_live(blocks, run)
        return carry

    lax.fori_loop(0, count, body, 0)


def table_scratch(count, points):
    tiles = points // LANES
    return [
        pltpu.VMEM((tiles, count, LANES), jnp.float32),
        pltpu.VMEM((tiles, DEG * count, LANES), jnp.float32),
        pltpu.VMEM((tiles, DEG * count, LANES), jnp.float32),
        pltpu.VMEM((S, LANES), jnp.float32),
    ]


def table_cost(count, points):
    cells = count * points * S
    return pl.CostEstimate(flops=cells * 3 * S * 2, bytes_accessed=cells, transcendentals=cells)


def moments_call(first, count, shared, wd=None, phi=None, dens=None, w=None):
    points = shared[-1].shape[2]
    fresh = wd is None
    out = [jax.ShapeDtypeStruct((count, 3 * S // 2, LANES), jnp.bfloat16)]
    args = list(shared)
    if fresh:
        out.append(jax.ShapeDtypeStruct((3, points), jnp.float32))
        args += [phi, dens, w]
    else:
        args += [wd]
    return pl.pallas_call(
        functools.partial(moments_kernel, first, count, fresh),
        out_shape=out,
        in_specs=[SMEM] * 4 + [VMEM] * (len(args) - 4),
        out_specs=[VMEM] * len(out),
        scratch_shapes=table_scratch(count, points),
        cost_estimate=table_cost(count, points),
        name="moments",
    )(*args)


def field_kernel(first, count, carried, last, *refs):
    (atoms_ref, pos_ref, blocks_ref, widths_ref, pts_ref, tab_ref), refs = refs[:6], refs[6:]
    if carried:
        acc_in, refs = refs[0], refs[1:]
    if last:
        (
            phi_ref, w_ref, marks_ref, flip_ref,
            out_ref, dist_ref, polar_ref, side_ref, scale_ref, acc_ref, oper_ref,
        ) = refs
    else:
        acc_ref, dist_ref, polar_ref, side_ref, scale_ref = refs
    points = pts_ref.shape[2]
    prepare(first, count, atoms_ref, pos_ref, pts_ref, dist_ref, polar_ref, side_ref)
    prepare_shells(widths_ref, scale_ref)
    acc_ref[...] = acc_in[...] if carried else jnp.zeros_like(acc_ref)

    def body(k, carry):
        blocks = blocks_ref[atoms_ref[first + k]]

        def run(live):
            half = live // 2
            middle, scale = shell_columns(blocks, live, scale_ref)
            table = tab_ref[k].astype(jnp.float32)
            lines = []
            for c in range(3):
                block = table[c * (S // 2) : c * (S // 2) + half]
                lines += [block[:, :S], block[:, S:]]
            left = jnp.concatenate(lines, axis=0).astype(jnp.bfloat16)
            for start in range(0, points, 256):
                t = start // LANES
                right = jnp.concatenate(
                    [angular_tile(k, count, t + d, polar_ref, side_ref) for d in range(2)], axis=1
                )
                spread = jnp.dot(left, right, preferred_element_type=jnp.float32)
                for d in range(2):
                    here = pl.ds(start + d * LANES, LANES)
                    radial = radial_tile(k, t + d, middle, scale, dist_ref)
                    for c in range(3):
                        sums = acc_ref[pl.ds(8 * c, 8), here]
                        for r in range(0, live, 8):
                            at = c * live + r
                            sums += radial[r : r + 8] * spread[at : at + 8, d * LANES : (d + 1) * LANES]
                        acc_ref[pl.ds(8 * c, 8), here] = sums

        by_live(blocks, run)
        return carry

    lax.fori_loop(0, count, body, 0)
    if last:
        piece = phi_ref.shape[1] // 2
        third = piece // 3
        quads = {}
        for c in range(3):
            for start in range(0, points, 256):
                here = pl.ds(start, 256)
                total = jnp.sum(acc_ref[pl.ds(8 * c, 8), here], axis=0, keepdims=True)
                wide = phi_ref[0, :, here].astype(jnp.float32)
                oper_ref[:, here] = (wide * (w_ref[:, here] * total)).astype(jnp.bfloat16)
            for x in range(2):
                for y in range(2):
                    quads[c, x, y] = lax.dot_general(
                        oper_ref[pl.ds(x * piece, piece), :],
                        phi_ref[0, pl.ds(y * piece, piece), :],
                        NT,
                        preferred_element_type=jnp.float32,
                    )
        for x in range(2):
            for y in range(2):
                q0, q1, q2 = (quads[c, x, y] for c in range(3))
                marks = jnp.concatenate(
                    [marks_ref[x], marks_ref[y], jnp.zeros((third - 16, third), jnp.float32)], axis=0
                )
                parts = [q2[b * third : (b + 1) * third, 2 * third :] for b in range(3)] + [marks]
                blocks = [
                    jnp.concatenate([q0, q2[:, :third]], axis=1),
                    jnp.concatenate([q1, q2[:, third : 2 * third]], axis=1),
                    jnp.concatenate(parts, axis=1),
                ]
                packed = jnp.concatenate(blocks, axis=0).astype(jnp.bfloat16)
                out_ref[y ^ flip_ref[0], x ^ flip_ref[1]] = packed


def field_call(first, count, shared, tables, acc=None, ends=None):
    points = shared[-1].shape[2]
    last = ends is not None
    args = list(shared) + [tables] + ([] if acc is None else [acc])
    plain = len(args)
    scratch = table_scratch(count, points)
    if last:
        args += ends
        third = ends[0].shape[1] // 6
        out = jax.ShapeDtypeStruct((2, 2, 7 * third, LANES), jnp.bfloat16)
        scratch += [pltpu.VMEM((24, points), jnp.float32), pltpu.VMEM(ends[0].shape[1:], jnp.bfloat16)]
    else:
        out = jax.ShapeDtypeStruct((24, points), jnp.float32)
    specs = [SMEM] * 4 + [VMEM] * (plain - 4)
    if last:
        specs += [VMEM] * 3 + [SMEM]
    return pl.pallas_call(
        functools.partial(field_kernel, first, count, acc is not None, last),
        out_shape=out,
        in_specs=specs,
        out_specs=VMEM,
        scratch_shapes=scratch,
        cost_estimate=table_cost(count, points),
        name="field",
    )(*args)


def place_kernel(pieces, carried, piece, tile, *refs):
    stacks, refs = refs[:pieces], refs[pieces:]
    if carried:
        acc_in, refs = refs[0], refs[1:]
    out_ref, rows_ref, wide_ref = refs
    third = piece // 3
    group = 4
    total = rows_ref.shape[1] // piece
    lane = lax.broadcasted_iota(jnp.int32, (piece, LANES), 1)
    sub = lax.broadcasted_iota(jnp.int32, (tile, LANES), 0)
    per = total // pieces
    for first in range(0, total, group):
        strips = []
        for g in range(first, first + group):
            ref, at = stacks[g // per], g % per
            tail = ref[at, pl.ds(2 * piece, third), :].astype(jnp.float32)
            marks = tail[: third // 2, 3 * third :]
            row_mark = marks[0:3] * 32.0 + marks[3:6]
            col_mark = marks[8:11] * 32.0 + marks[11:14]
            strips += [row_mark[b : b + 1] for b in range(3)]
            flat = jnp.concatenate([col_mark[b : b + 1] for b in range(3)] + [col_mark[0:1]], axis=1)
            column = jnp.transpose(jnp.broadcast_to(flat, (LANES, LANES)))[:piece].astype(jnp.int32)
            hits = jnp.concatenate(
                [
                    (column == lane + u).astype(jnp.float32).astype(jnp.bfloat16)
                    for u in range(0, tile, LANES)
                ],
                axis=1,
            )
            upper = ref[at, pl.ds(0, piece), :].astype(jnp.float32)
            lower = ref[at, pl.ds(piece, piece), :].astype(jnp.float32)
            rest = jnp.concatenate([tail[:, b * third : (b + 1) * third] for b in range(3)], axis=0)
            shared = jnp.concatenate([upper[:, piece:], lower[:, piece:], rest], axis=1)
            quads = jnp.concatenate([upper[:, :piece], lower[:, :piece], shared], axis=0)
            spread = jnp.dot(
                quads.astype(jnp.bfloat16), hits, preferred_element_type=jnp.float32
            ).astype(jnp.bfloat16)
            for c in range(3):
                wide_ref[c, pl.ds(g * piece, piece), :] = spread[c * piece : (c + 1) * piece]
        strip = jnp.concatenate(strips, axis=1).astype(jnp.int32)
        for start in range(0, group * piece, LANES):
            rows_ref[:, pl.ds(first * piece + start, LANES)] = (
                (sub == strip[:, start : start + LANES]).astype(jnp.float32).astype(jnp.bfloat16)
            )

    step = 256

    def body(i, carry):
        c, t = i // (tile // step), (i % (tile // step)) * step
        here = pl.ds(pl.multiple_of(t, step), step)
        value = jnp.dot(rows_ref[here, :], wide_ref[c], preferred_element_type=jnp.float32)
        if carried:
            value += acc_in[c, here, :]
        out_ref[c, here, :] = value.astype(out_ref.dtype)
        return carry

    lax.fori_loop(0, 3 * (tile // step), body, 0)


def place_call(stacks, piece, tile, acc=None, final=True):
    total = sum(stack.shape[0] for stack in stacks)
    depth = total * piece
    args = list(stacks) + ([] if acc is None else [acc])
    return pl.pallas_call(
        functools.partial(place_kernel, len(stacks), acc is not None, piece, tile),
        out_shape=jax.ShapeDtypeStruct((3, tile, tile), jnp.bfloat16 if final else jnp.float32),
        in_specs=[VMEM] * len(args),
        out_specs=VMEM,
        scratch_shapes=[
            pltpu.VMEM((tile, depth), jnp.bfloat16),
            pltpu.VMEM((3, depth, tile), jnp.bfloat16),
        ],
        input_output_aliases={} if acc is None or final else {len(stacks): 0},
        compiler_params=pltpu.CompilerParams(vmem_limit_bytes=28 << 20),
        cost_estimate=pl.CostEstimate(
            flops=2 * 3 * depth * tile * tile, bytes_accessed=12 * tile * tile, transcendentals=0
        ),
        name="place",
    )(*args)


def apply_green(charges, kernels):
    shaped = charges.astype(jnp.bfloat16).reshape(-1, 3, S, DEG, DEG)
    kernel_rows = kernels.reshape(-1, DEG, S, S)
    result = jnp.einsum(
        "xast,xctam->xcsam", kernel_rows, shaped, preferred_element_type=jnp.float32
    )
    return result.astype(jnp.bfloat16).reshape(-1, 3 * S * DEG * DEG)


def swap(value, axis, mask=1):
    size = lax.axis_size(axis)
    return lax.ppermute(value, axis, [(i, i ^ mask) for i in range(size)])


def plane_atoms(owners, row, col):
    flips = jnp.arange(4)
    inner = ((flips & 1) ^ row) * 2 + ((flips >> 1) ^ col)
    return (jnp.arange(owners)[None, :] * 4 + inner[:, None]).reshape(-1)


def on_device(
    basis_values,
    density_matrix,
    points,
    weights,
    intersection,
    basis_index,
    atom_positions,
    shell_blocks,
    shell_widths,
    green,
):
    atoms = intersection[0]
    labels = basis_index[0]
    owners = lax.axis_size("batch")
    parts = lax.axis_size("row")
    sides = lax.axis_size("col")
    row, col = lax.axis_index("row"), lax.axis_index("col")
    count = atoms.shape[0]
    slots = (count + owners - 1) // owners
    holding = green.shape[0]
    every_atom = atom_positions.shape[1]
    width = 3 * S * DEG * DEG
    lines = width // LANES
    highest = lax.Precision.HIGHEST
    dense = count == every_atom and holding == parts * sides
    if dense:
        atoms = plane_atoms(owners, row, col)
    group = count // 4
    shared = (atoms, atom_positions, shell_blocks, shell_widths, points)

    def moments_of(place, weighted):
        return moments_call(place * group, group, shared, wd=weighted)[0]

    third, weighted = moments_call(
        3 * group, group, shared, phi=basis_values, dens=density_matrix, w=weights
    )
    if dense:
        from_third = swap(third, "col")
        first = moments_of(1, weighted) + from_third
        from_first = swap(first, "row")
        from_second = swap(moments_of(2, weighted), "col")
        held = (
            moments_of(0, weighted).astype(jnp.float32)
            + from_second.astype(jnp.float32)
            + from_first.astype(jnp.float32)
        ).astype(jnp.bfloat16)
        shares = lax.all_to_all(held, "batch", split_axis=0, concat_axis=0, tiled=True)
        charges = jnp.sum(shares.astype(jnp.float32), axis=0)
        kernels = lax.dynamic_index_in_dim(green, row * sides + col, 0, keepdims=True)
        mine = apply_green(charges.reshape(1, width), kernels).reshape(1, lines, LANES)
        own = lax.all_to_all(
            jnp.broadcast_to(mine, (owners, lines, LANES)),
            "batch",
            split_axis=0,
            concat_axis=0,
            tiled=True,
        )
        beside = swap(own, "row")
        tables = [own, beside, swap(own, "col"), swap(beside, "col")]
        here = lax.axis_index("batch")
        plane = jnp.stack(
            [lax.dynamic_index_in_dim(table, here, 0, keepdims=False) for table in tables]
        )
        places = [(j // sides ^ row) + 2 * (j % sides ^ col) for j in range(holding)]
        potential = jnp.concatenate(
            [lax.dynamic_index_in_dim(plane, place, 0) for place in places]
        ).reshape(holding, width)
    else:
        moments = jnp.concatenate([moments_of(place, weighted) for place in range(3)] + [third])
        moments = moments.astype(jnp.float32).reshape(count, width)
        home = atoms // holding
        local_slot = atoms % holding
        order = jnp.arange(count)
        before = (home[None, :] == home[:, None]) & (order[None, :] < order[:, None])
        place = home * slots + jnp.sum(before, axis=1)
        routing = jnp.arange(owners * slots)[:, None] == place[None, :]
        outgoing = jnp.dot(routing.astype(jnp.float32), moments, precision=highest).reshape(
            owners, slots, width
        )
        tags = (jnp.sum(jnp.where(routing, local_slot[None, :] + 1, 0), axis=1) - 1).reshape(
            owners, slots
        )
        incoming, sources = (
            lax.all_to_all(outgoing, "batch", split_axis=0, concat_axis=0, tiled=True),
            lax.all_to_all(tags, "batch", split_axis=0, concat_axis=0, tiled=True),
        )
        collect = jnp.arange(holding)[:, None] == sources.reshape(1, owners * slots)
        partial_value = jnp.dot(
            collect.astype(jnp.float32), incoming.reshape(owners * slots, width), precision=highest
        )
        totals = lax.psum(partial_value, ("row", "col"))
        potential = apply_green(totals, green)
        back = jnp.dot(
            collect.T.astype(jnp.bfloat16), potential, preferred_element_type=jnp.float32
        ).astype(jnp.bfloat16)
        returned = lax.all_to_all(
            back.reshape(owners, slots, width), "batch", split_axis=0, concat_axis=0, tiled=True
        )
        table = jnp.dot(
            routing.T.astype(jnp.bfloat16),
            returned.reshape(owners * slots, width),
            preferred_element_type=jnp.float32,
        )
        table = table.astype(jnp.bfloat16).reshape(count, lines, LANES)
        tables = [table[place * group : (place + 1) * group] for place in range(4)]
    piece = labels.shape[0] // parts
    tile = NB // parts
    inner = labels.reshape(parts, 3, piece // 3) - jnp.arange(parts)[:, None, None] * tile
    marks = jnp.concatenate([inner // 32, inner % 32, inner[:, :2] * 0], axis=1)
    marks = marks.astype(jnp.float32)
    field = None
    for place in (0, 2, 1):
        field = field_call(place * group, group, shared, tables[place], field)
    ends = [basis_values, weights, marks, jnp.stack([col, row])]
    load = field_call(3 * group, group, shared, tables[3], field, ends)
    plane = ("row", "col")
    across = [(i, i ^ 3) for i in range(parts * sides)]
    diagonal = lax.ppermute(load[1, 1:], plane, across)
    plane_load = jnp.concatenate(
        [load[0, :1], swap(load[1, :1], "col"), swap(load[0, 1:], "row"), diagonal], axis=0
    )
    if owners <= 8:
        near = [plane_load] + [swap(plane_load, "batch", m) for m in range(2, owners, 2)]
        far = [swap(line, "batch") for line in near]
        total = None
        for first in range(0, len(near), 2):
            for lines in (near, far):
                last = lines is far and first + 2 >= len(near)
                total = place_call(lines[first : first + 2], piece, tile, total, final=last)
        hamiltonian = total
    else:
        everyone = lax.all_gather(plane_load, "batch", axis=0)
        chunk = 4
        everyone = everyone.reshape((owners // chunk, chunk * 4) + plane_load.shape[1:])

        def add(total, item):
            return place_call([item], piece, tile, total, final=False), None

        total, _ = lax.scan(add, jnp.zeros((3, tile, tile), jnp.float32), everyone)
        hamiltonian = total.astype(jnp.bfloat16)
    return (potential, hamiltonian)


def solution(mesh):
    return jax.shard_map(
        on_device,
        mesh=mesh,
        in_specs=(
            P(("batch", "row", "col"), None, None),
            P(("batch", "row", "col"), None, None, None),
            P(("batch", "row", "col"), None, None),
            P(("batch", "row", "col"), None),
            P(("batch", "row", "col"), None),
            P(("batch", "row", "col"), None),
            P(),
            P(),
            P(),
            P("batch", None, None),
        ),
        out_specs=(P("batch", None), P(None, "row", "col")),
        check_vma=False,
    )
```

```python
import functools

import jax
import jax.numpy as jnp
from jax import lax
from jax.experimental import pallas as pl
from jax.experimental.pallas import tpu as pltpu
from jax.sharding import PartitionSpec as P


S = 64
DEG = 8
NB = 1536
LANES = 128
FAR = 1.0e6
LOG2E = 1.4426950408889634
NT = (((1,), (1,)), ((), ()))
SMEM = pl.BlockSpec(memory_space=pltpu.SMEM)
VMEM = pl.BlockSpec(memory_space=pltpu.VMEM)


def prepare(chosen, atoms_ref, pos_ref, pts_ref, dist_ref, polar_ref, side_ref):
    count = len(chosen)
    rows = lax.broadcasted_iota(jnp.int32, (count, LANES), 0)
    centre = []
    for axis in range(3):
        column = jnp.zeros((count, LANES), jnp.float32)
        for k, place in enumerate(chosen):
            column = jnp.where(rows == k, pos_ref[axis, atoms_ref[place]], column)
        centre.append(column)
    for t in range(pts_ref.shape[2] // LANES):
        here = pl.ds(t * LANES, LANES)
        delta = [pts_ref[0, pl.ds(axis, 1), here] - centre[axis] for axis in range(3)]
        square = delta[0] * delta[0] + delta[1] * delta[1] + delta[2] * delta[2] + 0.01
        inverse = lax.rsqrt(square)
        dist_ref[t] = square * inverse
        for ladder, u in ((polar_ref, delta[2] * inverse), (side_ref, delta[0] * inverse)):
            older, old = jnp.ones_like(u), u
            ladder[t, pl.ds(0, count), :] = older
            ladder[t, pl.ds(count, count), :] = old
            for order in range(2, DEG):
                older, old = old, 2.0 * u * old - older
                ladder[t, pl.ds(order * count, count), :] = old


def prepare_shells(widths_ref, scale_ref):
    rows = lax.broadcasted_iota(jnp.int32, (8, LANES), 0)
    for start in range(0, S, 8):
        column = jnp.zeros((8, LANES), jnp.float32)
        for j in range(8):
            place = start + j
            shell = 2 * place if place < S // 2 else 2 * place - (S - 1)
            column = jnp.where(rows == j, widths_ref[shell], column)
        scale_ref[pl.ds(start, 8), :] = -LOG2E / (column * column)


def shell_columns(blocks, live, scale_ref):
    half = live // 2
    place = lax.broadcasted_iota(jnp.int32, (live, LANES), 0)
    shell = jnp.where(place < half, 2 * place, 2 * place - (live - 1))
    middle = jnp.where(shell < 8 * blocks, shell.astype(jnp.float32) * (4.0 / S), FAR)
    scale = jnp.concatenate(
        [scale_ref[pl.ds(0, half), :], scale_ref[pl.ds(S // 2, half), :]], axis=0
    )
    return middle, scale


def angular_tile(k, count, t, polar_ref, side_ref):
    side = side_ref[t, pl.ds(k, DEG, stride=count), :]
    return jnp.concatenate(
        [
            polar_ref[t, pl.ds(order * count + k, DEG, stride=0), :] * side
            for order in range(DEG)
        ],
        axis=0,
    ).astype(jnp.bfloat16)


def radial_tile(k, t, middle, scale, dist_ref):
    dist = dist_ref[t, pl.ds(k, 8, stride=0), :]
    gap = jnp.concatenate([dist] * (middle.shape[0] // 8), axis=0) - middle
    return jnp.exp2(gap * (gap * scale))


def by_live(blocks, run):
    for live in range(16, S + 1, 16):

        @pl.when((blocks * 8 > live - 16) & (blocks * 8 <= live))
        def _(live=live):
            run(live)


def moments_kernel(first, count, fresh, *refs):
    if fresh:
        (
            atoms_ref, pos_ref, blocks_ref, widths_ref, pts_ref, phi_ref, dens_ref, w_ref,
            out_ref, wd_ref, dist_ref, polar_ref, side_ref, scale_ref,
        ) = refs
    else:
        (
            atoms_ref, pos_ref, blocks_ref, widths_ref, pts_ref, wd_ref,
            out_ref, dist_ref, polar_ref, side_ref, scale_ref,
        ) = refs
    points = pts_ref.shape[2]
    if fresh:
        for start in range(0, points, 256):
            here = pl.ds(start, 256)
            phi = phi_ref[0, :, here]
            wide = phi.astype(jnp.float32)
            for c in range(3):
                product = jnp.dot(dens_ref[0, c], phi, preferred_element_type=jnp.float32)
                density = jnp.sum(wide * product, axis=0, keepdims=True)
                wd_ref[pl.ds(c, 1), here] = w_ref[:, here] * density
    prepare(range(first, first + count), atoms_ref, pos_ref, pts_ref, dist_ref, polar_ref, side_ref)
    prepare_shells(widths_ref, scale_ref)

    def body(k, carry):
        blocks = blocks_ref[atoms_ref[first + k]]

        def run(live):
            middle, scale = shell_columns(blocks, live, scale_ref)
            total = jnp.zeros((3 * live, S), jnp.float32)
            for start in range(0, points, 256):
                scaled, angles = [[], [], []], []
                for inner in (start, start + LANES):
                    t = inner // LANES
                    radial = radial_tile(k, t, middle, scale, dist_ref).astype(jnp.bfloat16)
                    angles.append(angular_tile(k, count, t, polar_ref, side_ref))
                    for c in range(3):
                        row = jnp.broadcast_to(wd_ref[pl.ds(c, 1), pl.ds(inner, LANES)], (16, LANES))
                        row = jnp.concatenate([row.astype(jnp.bfloat16)] * (live // 16), axis=0)
                        scaled[c].append(radial * row)
                left = jnp.concatenate([jnp.concatenate(s, axis=1) for s in scaled], axis=0)
                right = jnp.concatenate(angles, axis=1)
                total += lax.dot_general(left, right, NT, preferred_element_type=jnp.float32)
            half = live // 2
            for c in range(3):
                even = total[c * live : c * live + half]
                odd = total[c * live + half : (c + 1) * live]
                block = jnp.concatenate([even, odd], axis=1)
                if live < S:
                    rest = jnp.zeros((S // 2 - half, LANES), jnp.float32)
                    block = jnp.concatenate([block, rest], axis=0)
                out_ref[k, pl.ds(c * (S // 2), S // 2), :] = block.astype(out_ref.dtype)

        by_live(blocks, run)
        return carry

    lax.fori_loop(0, count, body, 0)


def table_scratch(count, points):
    tiles = points // LANES
    return [
        pltpu.VMEM((tiles, count, LANES), jnp.float32),
        pltpu.VMEM((tiles, DEG * count, LANES), jnp.float32),
        pltpu.VMEM((tiles, DEG * count, LANES), jnp.float32),
        pltpu.VMEM((S, LANES), jnp.float32),
    ]


def table_cost(count, points):
    cells = count * points * S
    return pl.CostEstimate(flops=cells * 3 * S * 2, bytes_accessed=cells, transcendentals=cells)


def moments_call(first, count, shared, wd=None, phi=None, dens=None, w=None):
    points = shared[-1].shape[2]
    fresh = wd is None
    out = [jax.ShapeDtypeStruct((count, 3 * S // 2, LANES), jnp.bfloat16)]
    args = list(shared)
    if fresh:
        out.append(jax.ShapeDtypeStruct((3, points), jnp.float32))
        args += [phi, dens, w]
    else:
        args += [wd]
    return pl.pallas_call(
        functools.partial(moments_kernel, first, count, fresh),
        out_shape=out,
        in_specs=[SMEM] * 4 + [VMEM] * (len(args) - 4),
        out_specs=[VMEM] * len(out),
        scratch_shapes=table_scratch(count, points),
        cost_estimate=table_cost(count, points),
        name="moments",
    )(*args)


def field_kernel(firsts, size, carried, kept, last, *refs):
    (atoms_ref, pos_ref, blocks_ref, widths_ref, flip_ref, pts_ref), refs = refs[:6], refs[6:]
    tabs, refs = refs[: len(firsts)], refs[len(firsts) :]
    count = len(firsts) * size
    if carried:
        acc_in, refs = refs[0], refs[1:]
    if kept == 2:
        plane_in, refs = refs[0], refs[1:]
    if last:
        (phi_ref, w_ref, marks_ref, out_ref), refs = refs[:4], refs[4:]
    else:
        acc_ref, refs = refs[0], refs[1:]
    if kept:
        plane_ref, refs = refs[0], refs[1:]
        rows = [tab[flip_ref[2]] for tab in tabs]
        if kept == 2:
            rows = [plane_in[0]] + rows
        for order, value in enumerate(rows):
            plane_ref[order if len(rows) == 1 else order ^ flip_ref[0]] = value
    dist_ref, polar_ref, side_ref, scale_ref = refs[:4]
    if last:
        acc_ref, oper_ref = refs[4:]
    points = pts_ref.shape[2]
    chosen = [first + k for first in firsts for k in range(size)]
    prepare(chosen, atoms_ref, pos_ref, pts_ref, dist_ref, polar_ref, side_ref)
    prepare_shells(widths_ref, scale_ref)
    acc_ref[...] = acc_in[...] if carried else jnp.zeros_like(acc_ref)

    def body(i, carry, tab_ref, first, base):
        k = base + i
        blocks = blocks_ref[atoms_ref[first + i]]

        def run(live):
            half = live // 2
            middle, scale = shell_columns(blocks, live, scale_ref)
            table = tab_ref[i].astype(jnp.float32)
            lines = []
            for c in range(3):
                block = table[c * (S // 2) : c * (S // 2) + half]
                lines += [block[:, :S], block[:, S:]]
            left = jnp.concatenate(lines, axis=0).astype(jnp.bfloat16)
            for start in range(0, points, 256):
                t = start // LANES
                right = jnp.concatenate(
                    [angular_tile(k, count, t + d, polar_ref, side_ref) for d in range(2)], axis=1
                )
                spread = jnp.dot(left, right, preferred_element_type=jnp.float32)
                for d in range(2):
                    here = pl.ds(start + d * LANES, LANES)
                    radial = radial_tile(k, t + d, middle, scale, dist_ref)
                    for c in range(3):
                        sums = acc_ref[pl.ds(8 * c, 8), here]
                        for r in range(0, live, 8):
                            at = c * live + r
                            sums += radial[r : r + 8] * spread[at : at + 8, d * LANES : (d + 1) * LANES]
                        acc_ref[pl.ds(8 * c, 8), here] = sums

        by_live(blocks, run)
        return carry

    for order, first in enumerate(firsts):
        group = functools.partial(body, tab_ref=tabs[order], first=first, base=order * size)
        lax.fori_loop(0, size, group, 0)
    if last:
        piece = phi_ref.shape[1] // 2
        third = piece // 3
        quads = {}
        for c in range(3):
            for start in range(0, points, 256):
                here = pl.ds(start, 256)
                total = jnp.sum(acc_ref[pl.ds(8 * c, 8), here], axis=0, keepdims=True)
                wide = phi_ref[0, :, here].astype(jnp.float32)
                oper_ref[:, here] = (wide * (w_ref[:, here] * total)).astype(jnp.bfloat16)
            for x in range(2):
                for y in range(2):
                    quads[c, x, y] = lax.dot_general(
                        oper_ref[pl.ds(x * piece, piece), :],
                        phi_ref[0, pl.ds(y * piece, piece), :],
                        NT,
                        preferred_element_type=jnp.float32,
                    )
        for x in range(2):
            for y in range(2):
                q0, q1, q2 = (quads[c, x, y] for c in range(3))
                marks = jnp.concatenate(
                    [marks_ref[x], marks_ref[y], jnp.zeros((third - 16, third), jnp.float32)], axis=0
                )
                parts = [q2[b * third : (b + 1) * third, 2 * third :] for b in range(3)] + [marks]
                blocks = [
                    jnp.concatenate([q0, q2[:, :third]], axis=1),
                    jnp.concatenate([q1, q2[:, third : 2 * third]], axis=1),
                    jnp.concatenate(parts, axis=1),
                ]
                packed = jnp.concatenate(blocks, axis=0).astype(jnp.bfloat16)
                out_ref[y ^ flip_ref[0], x ^ flip_ref[1]] = packed


def field_call(firsts, size, shared, flip, tables, acc=None, plane=None, keep=True, ends=None):
    points = shared[-1].shape[2]
    last = ends is not None
    count = len(firsts) * size
    args = list(shared[:-1]) + [flip, shared[-1]] + list(tables)
    args += [] if acc is None else [acc]
    args += [] if plane is None else [plane]
    scratch = table_scratch(count, points)
    if last:
        args += ends
        third = ends[0].shape[1] // 6
        out = [jax.ShapeDtypeStruct((2, 2, 7 * third, LANES), jnp.bfloat16)]
        scratch += [pltpu.VMEM((24, points), jnp.float32), pltpu.VMEM(ends[0].shape[1:], jnp.bfloat16)]
    else:
        out = [jax.ShapeDtypeStruct((24, points), jnp.float32)]
    kept = 0
    if keep:
        kept = 1 if plane is None else 2
        rows = len(firsts) if plane is None else 2
        out.append(jax.ShapeDtypeStruct((rows,) + tables[0].shape[1:], jnp.bfloat16))
    return pl.pallas_call(
        functools.partial(field_kernel, firsts, size, acc is not None, kept, last),
        out_shape=out,
        in_specs=[SMEM] * 5 + [VMEM] * (len(args) - 5),
        out_specs=[VMEM] * len(out),
        scratch_shapes=scratch,
        cost_estimate=table_cost(count, points),
        name="field",
    )(*args)


def place_kernel(pieces, carried, piece, tile, *refs):
    stacks, refs = refs[:pieces], refs[pieces:]
    if carried:
        acc_in, refs = refs[0], refs[1:]
    out_ref, rows_ref, wide_ref = refs
    third = piece // 3
    group = 4
    total = rows_ref.shape[1] // piece
    lane = lax.broadcasted_iota(jnp.int32, (piece, LANES), 1)
    sub = lax.broadcasted_iota(jnp.int32, (tile, LANES), 0)
    per = total // pieces
    for first in range(0, total, group):
        strips = []
        for g in range(first, first + group):
            ref, at = stacks[g // per], g % per
            tail = ref[at, pl.ds(2 * piece, third), :].astype(jnp.float32)
            marks = tail[: third // 2, 3 * third :]
            row_mark = marks[0:3] * 32.0 + marks[3:6]
            col_mark = marks[8:11] * 32.0 + marks[11:14]
            strips += [row_mark[b : b + 1] for b in range(3)]
            flat = jnp.concatenate([col_mark[b : b + 1] for b in range(3)] + [col_mark[0:1]], axis=1)
            column = jnp.transpose(jnp.broadcast_to(flat, (LANES, LANES)))[:piece].astype(jnp.int32)
            hits = jnp.concatenate(
                [
                    (column == lane + u).astype(jnp.float32).astype(jnp.bfloat16)
                    for u in range(0, tile, LANES)
                ],
                axis=1,
            )
            upper = ref[at, pl.ds(0, piece), :].astype(jnp.float32)
            lower = ref[at, pl.ds(piece, piece), :].astype(jnp.float32)
            rest = jnp.concatenate([tail[:, b * third : (b + 1) * third] for b in range(3)], axis=0)
            shared = jnp.concatenate([upper[:, piece:], lower[:, piece:], rest], axis=1)
            quads = jnp.concatenate([upper[:, :piece], lower[:, :piece], shared], axis=0)
            spread = jnp.dot(
                quads.astype(jnp.bfloat16), hits, preferred_element_type=jnp.float32
            ).astype(jnp.bfloat16)
            for c in range(3):
                wide_ref[c, pl.ds(g * piece, piece), :] = spread[c * piece : (c + 1) * piece]
        strip = jnp.concatenate(strips, axis=1).astype(jnp.int32)
        for start in range(0, group * piece, LANES):
            rows_ref[:, pl.ds(first * piece + start, LANES)] = (
                (sub == strip[:, start : start + LANES]).astype(jnp.float32).astype(jnp.bfloat16)
            )

    step = 256

    def body(i, carry):
        c, t = i // (tile // step), (i % (tile // step)) * step
        here = pl.ds(pl.multiple_of(t, step), step)
        value = jnp.dot(rows_ref[here, :], wide_ref[c], preferred_element_type=jnp.float32)
        if carried:
            value += acc_in[c, here, :]
        out_ref[c, here, :] = value.astype(out_ref.dtype)
        return carry

    lax.fori_loop(0, 3 * (tile // step), body, 0)


def place_call(stacks, piece, tile, acc=None, final=True):
    total = sum(stack.shape[0] for stack in stacks)
    depth = total * piece
    args = list(stacks) + ([] if acc is None else [acc])
    return pl.pallas_call(
        functools.partial(place_kernel, len(stacks), acc is not None, piece, tile),
        out_shape=jax.ShapeDtypeStruct((3, tile, tile), jnp.bfloat16 if final else jnp.float32),
        in_specs=[VMEM] * len(args),
        out_specs=VMEM,
        scratch_shapes=[
            pltpu.VMEM((tile, depth), jnp.bfloat16),
            pltpu.VMEM((3, depth, tile), jnp.bfloat16),
        ],
        input_output_aliases={} if acc is None or final else {len(stacks): 0},
        compiler_params=pltpu.CompilerParams(vmem_limit_bytes=28 << 20),
        cost_estimate=pl.CostEstimate(
            flops=8 * 3 * depth * tile * tile, bytes_accessed=12 * tile * tile, transcendentals=0
        ),
        name="place",
    )(*args)


def apply_green(charges, kernels):
    shaped = charges.astype(jnp.bfloat16).reshape(-1, 3, S, DEG, DEG)
    kernel_rows = kernels.reshape(-1, DEG, S, S)
    result = jnp.einsum(
        "xast,xctam->xcsam", kernel_rows, shaped, preferred_element_type=jnp.float32
    )
    return result.astype(jnp.bfloat16).reshape(-1, 3 * S * DEG * DEG)


def swap(value, axis, mask=1):
    size = lax.axis_size(axis)
    return lax.ppermute(value, axis, [(i, i ^ mask) for i in range(size)])


def plane_atoms(owners, row, col):
    flips = jnp.arange(4)
    inner = ((flips & 1) ^ row) * 2 + ((flips >> 1) ^ col)
    return (jnp.arange(owners)[None, :] * 4 + inner[:, None]).reshape(-1)


def on_device(
    basis_values,
    density_matrix,
    points,
    weights,
    intersection,
    basis_index,
    atom_positions,
    shell_blocks,
    shell_widths,
    green,
):
    atoms = intersection[0]
    labels = basis_index[0]
    owners = lax.axis_size("batch")
    parts = lax.axis_size("row")
    sides = lax.axis_size("col")
    row, col = lax.axis_index("row"), lax.axis_index("col")
    count = atoms.shape[0]
    slots = (count + owners - 1) // owners
    holding = green.shape[0]
    every_atom = atom_positions.shape[1]
    width = 3 * S * DEG * DEG
    lines = width // LANES
    highest = lax.Precision.HIGHEST
    dense = count == every_atom and holding == parts * sides
    if dense:
        atoms = plane_atoms(owners, row, col)
    group = count // 4
    shared = (atoms, atom_positions, shell_blocks, shell_widths, points)

    def moments_of(place, weighted):
        return moments_call(place * group, group, shared, wd=weighted)[0]

    third, weighted = moments_call(
        3 * group, group, shared, phi=basis_values, dens=density_matrix, w=weights
    )
    if dense:
        from_third = swap(third, "col")
        first = moments_of(1, weighted) + from_third
        from_first = swap(first, "row")
        from_second = swap(moments_of(2, weighted), "col")
        held = (
            moments_of(0, weighted).astype(jnp.float32)
            + from_second.astype(jnp.float32)
            + from_first.astype(jnp.float32)
        ).astype(jnp.bfloat16)
        shares = lax.all_to_all(held, "batch", split_axis=0, concat_axis=0, tiled=True)
        charges = jnp.sum(shares.astype(jnp.float32), axis=0)
        kernels = lax.dynamic_index_in_dim(green, row * sides + col, 0, keepdims=True)
        mine = apply_green(charges.reshape(1, width), kernels).reshape(1, lines, LANES)
        own = lax.all_to_all(
            jnp.broadcast_to(mine, (owners, lines, LANES)),
            "batch",
            split_axis=0,
            concat_axis=0,
            tiled=True,
        )
        beside = swap(own, "row")
        across = swap(beside, "col")
        tables = [own, beside, swap(own, "col"), across]
    else:
        moments = jnp.concatenate([moments_of(place, weighted) for place in range(3)] + [third])
        moments = moments.astype(jnp.float32).reshape(count, width)
        home = atoms // holding
        local_slot = atoms % holding
        order = jnp.arange(count)
        before = (home[None, :] == home[:, None]) & (order[None, :] < order[:, None])
        place = home * slots + jnp.sum(before, axis=1)
        routing = jnp.arange(owners * slots)[:, None] == place[None, :]
        outgoing = jnp.dot(routing.astype(jnp.float32), moments, precision=highest).reshape(
            owners, slots, width
        )
        tags = (jnp.sum(jnp.where(routing, local_slot[None, :] + 1, 0), axis=1) - 1).reshape(
            owners, slots
        )
        incoming, sources = (
            lax.all_to_all(outgoing, "batch", split_axis=0, concat_axis=0, tiled=True),
            lax.all_to_all(tags, "batch", split_axis=0, concat_axis=0, tiled=True),
        )
        collect = jnp.arange(holding)[:, None] == sources.reshape(1, owners * slots)
        partial_value = jnp.dot(
            collect.astype(jnp.float32), incoming.reshape(owners * slots, width), precision=highest
        )
        totals = lax.psum(partial_value, ("row", "col"))
        potential = apply_green(totals, green)
        back = jnp.dot(
            collect.T.astype(jnp.bfloat16), potential, preferred_element_type=jnp.float32
        ).astype(jnp.bfloat16)
        returned = lax.all_to_all(
            back.reshape(owners, slots, width), "batch", split_axis=0, concat_axis=0, tiled=True
        )
        table = jnp.dot(
            routing.T.astype(jnp.bfloat16),
            returned.reshape(owners * slots, width),
            preferred_element_type=jnp.float32,
        )
        table = table.astype(jnp.bfloat16).reshape(count, lines, LANES)
        tables = [table[place * group : (place + 1) * group] for place in range(4)]
    piece = labels.shape[0] // parts
    tile = NB // parts
    inner = labels.reshape(parts, 3, piece // 3) - jnp.arange(parts)[:, None, None] * tile
    marks = jnp.concatenate([inner // 32, inner % 32, inner[:, :2] * 0], axis=1)
    marks = marks.astype(jnp.float32)
    flip = jnp.stack([col, row, lax.axis_index("batch")])
    ends = [basis_values, weights, marks]
    spread = functools.partial(field_call, size=group, shared=shared, flip=flip, keep=dense)
    field, *ours = spread((0, 2 * group), tables=[tables[0], tables[2]])
    field, *half = spread((group,), tables=[tables[1]], acc=field)
    load, *theirs = spread(
        (3 * group,), tables=[tables[3]], acc=field, plane=half[0] if half else None, ends=ends
    )
    if dense:
        ours, theirs = ours[0], theirs[0]
        potential = jnp.concatenate(
            [jnp.where(row == 0, ours, theirs), jnp.where(row == 0, theirs, ours)]
        ).reshape(holding, width)
    plane = ("row", "col")
    across = [(i, i ^ 3) for i in range(parts * sides)]
    diagonal = lax.ppermute(load[1, 1:], plane, across)
    plane_load = jnp.concatenate(
        [load[0, :1], swap(load[1, :1], "col"), swap(load[0, 1:], "row"), diagonal], axis=0
    )
    if owners <= 8:
        near, far = [plane_load], []
        for step in range(2, owners, 2):
            near.append(swap(plane_load, "batch", step))
        for line in near:
            far.append(swap(line, "batch"))
        total = None
        for first in range(0, len(near), 2):
            for lines in (near, far):
                last = lines is far and first + 2 >= len(near)
                total = place_call(lines[first : first + 2], piece, tile, total, final=last)
        hamiltonian = total
    else:
        everyone = lax.all_gather(plane_load, "batch", axis=0)
        chunk = 4
        everyone = everyone.reshape((owners // chunk, chunk * 4) + plane_load.shape[1:])

        def add(total, item):
            return place_call([item], piece, tile, total, final=False), None

        total, _ = lax.scan(add, jnp.zeros((3, tile, tile), jnp.float32), everyone)
        hamiltonian = total.astype(jnp.bfloat16)
    return (potential, hamiltonian)


def solution(mesh):
    return jax.shard_map(
        on_device,
        mesh=mesh,
        in_specs=(
            P(("batch", "row", "col"), None, None),
            P(("batch", "row", "col"), None, None, None),
            P(("batch", "row", "col"), None, None),
            P(("batch", "row", "col"), None),
            P(("batch", "row", "col"), None),
            P(("batch", "row", "col"), None),
            P(),
            P(),
            P(),
            P("batch", None, None),
        ),
        out_specs=(P("batch", None), P(None, "row", "col")),
        check_vma=False,
    )
```

```python
import functools

import jax
import jax.numpy as jnp
from jax import lax
from jax.experimental import pallas as pl
from jax.experimental.pallas import tpu as pltpu
from jax.sharding import PartitionSpec as P


S = 64
DEG = 8
NB = 1536
LANES = 128
FAR = 1.0e6
LOG2E = 1.4426950408889634
NT = (((1,), (1,)), ((), ()))
SMEM = pl.BlockSpec(memory_space=pltpu.SMEM)
VMEM = pl.BlockSpec(memory_space=pltpu.VMEM)


def atom_finder(group, atoms_ref):
    if isinstance(group, int):
        return lambda i: atoms_ref[group + i]
    stride, row_flip, col_flip = group
    base = lax.axis_index("col") ^ col_flip
    if row_flip is not None:
        base = base + (lax.axis_index("row") ^ row_flip) * 2
    return lambda i: base + i * stride


def prepare(chosen, pos_ref, pts_ref, dist_ref, polar_ref, side_ref):
    count = len(chosen)
    rows = lax.broadcasted_iota(jnp.int32, (count, LANES), 0)
    centre = []
    for axis in range(3):
        column = jnp.zeros((count, LANES), jnp.float32)
        for k, atom in enumerate(chosen):
            column = jnp.where(rows == k, pos_ref[axis, atom], column)
        centre.append(column)
    for t in range(pts_ref.shape[2] // LANES):
        here = pl.ds(t * LANES, LANES)
        delta = [pts_ref[0, pl.ds(axis, 1), here] - centre[axis] for axis in range(3)]
        square = delta[0] * delta[0] + delta[1] * delta[1] + delta[2] * delta[2] + 0.01
        inverse = lax.rsqrt(square)
        dist_ref[t] = square * inverse
        for ladder, u in ((polar_ref, delta[2] * inverse), (side_ref, delta[0] * inverse)):
            older, old = jnp.ones_like(u), u
            ladder[t, pl.ds(0, count), :] = older
            ladder[t, pl.ds(count, count), :] = old
            for order in range(2, DEG):
                older, old = old, 2.0 * u * old - older
                ladder[t, pl.ds(order * count, count), :] = old


def prepare_shells(widths_ref, scale_ref):
    rows = lax.broadcasted_iota(jnp.int32, (8, LANES), 0)
    for start in range(0, S, 8):
        column = jnp.zeros((8, LANES), jnp.float32)
        for j in range(8):
            place = start + j
            shell = 2 * place if place < S // 2 else 2 * place - (S - 1)
            column = jnp.where(rows == j, widths_ref[shell], column)
        scale_ref[pl.ds(start, 8), :] = -LOG2E / (column * column)


def shell_columns(blocks, live, scale_ref):
    half = live // 2
    place = lax.broadcasted_iota(jnp.int32, (live, LANES), 0)
    shell = jnp.where(place < half, 2 * place, 2 * place - (live - 1))
    middle = jnp.where(shell < 8 * blocks, shell.astype(jnp.float32) * (4.0 / S), FAR)
    scale = jnp.concatenate(
        [scale_ref[pl.ds(0, half), :], scale_ref[pl.ds(S // 2, half), :]], axis=0
    )
    return middle, scale


def angular_tile(k, count, t, polar_ref, side_ref):
    side = side_ref[t, pl.ds(k, DEG, stride=count), :]
    return jnp.concatenate(
        [
            polar_ref[t, pl.ds(order * count + k, DEG, stride=0), :] * side
            for order in range(DEG)
        ],
        axis=0,
    ).astype(jnp.bfloat16)


def radial_tile(k, t, middle, scale, dist_ref):
    dist = dist_ref[t, pl.ds(k, 8, stride=0), :]
    gap = jnp.concatenate([dist] * (middle.shape[0] // 8), axis=0) - middle
    return jnp.exp2(gap * (gap * scale))


def by_live(blocks, run):
    for live in range(16, S + 1, 16):

        @pl.when((blocks * 8 > live - 16) & (blocks * 8 <= live))
        def _(live=live):
            run(live)


def moments_kernel(group, count, fresh, *refs):
    if fresh:
        (
            atoms_ref, pos_ref, blocks_ref, widths_ref, pts_ref, phi_ref, dens_ref, w_ref,
            out_ref, wd_ref, dist_ref, polar_ref, side_ref, scale_ref,
        ) = refs
    else:
        (
            atoms_ref, pos_ref, blocks_ref, widths_ref, pts_ref, wd_ref,
            out_ref, dist_ref, polar_ref, side_ref, scale_ref,
        ) = refs
    points = pts_ref.shape[2]
    if fresh:
        for start in range(0, points, 256):
            here = pl.ds(start, 256)
            phi = phi_ref[0, :, here]
            wide = phi.astype(jnp.float32)
            for c in range(3):
                product = jnp.dot(dens_ref[0, c], phi, preferred_element_type=jnp.float32)
                density = jnp.sum(wide * product, axis=0, keepdims=True)
                wd_ref[pl.ds(c, 1), here] = w_ref[:, here] * density
    atom_at = atom_finder(group, atoms_ref)
    prepare([atom_at(i) for i in range(count)], pos_ref, pts_ref, dist_ref, polar_ref, side_ref)
    prepare_shells(widths_ref, scale_ref)

    def body(k, carry):
        blocks = blocks_ref[atom_at(k)]

        def run(live):
            middle, scale = shell_columns(blocks, live, scale_ref)
            total = jnp.zeros((3 * live, S), jnp.float32)
            for start in range(0, points, 256):
                scaled, angles = [[], [], []], []
                for inner in (start, start + LANES):
                    t = inner // LANES
                    radial = radial_tile(k, t, middle, scale, dist_ref).astype(jnp.bfloat16)
                    angles.append(angular_tile(k, count, t, polar_ref, side_ref))
                    for c in range(3):
                        row = jnp.broadcast_to(wd_ref[pl.ds(c, 1), pl.ds(inner, LANES)], (16, LANES))
                        row = jnp.concatenate([row.astype(jnp.bfloat16)] * (live // 16), axis=0)
                        scaled[c].append(radial * row)
                left = jnp.concatenate([jnp.concatenate(s, axis=1) for s in scaled], axis=0)
                right = jnp.concatenate(angles, axis=1)
                total += lax.dot_general(left, right, NT, preferred_element_type=jnp.float32)
            half = live // 2
            for c in range(3):
                even = total[c * live : c * live + half]
                odd = total[c * live + half : (c + 1) * live]
                block = jnp.concatenate([even, odd], axis=1)
                if live < S:
                    rest = jnp.zeros((S // 2 - half, LANES), jnp.float32)
                    block = jnp.concatenate([block, rest], axis=0)
                out_ref[k, pl.ds(c * (S // 2), S // 2), :] = block.astype(out_ref.dtype)

        by_live(blocks, run)
        return carry

    lax.fori_loop(0, count, body, 0)


def table_scratch(count, points):
    tiles = points // LANES
    return [
        pltpu.VMEM((tiles, count, LANES), jnp.float32),
        pltpu.VMEM((tiles, DEG * count, LANES), jnp.float32),
        pltpu.VMEM((tiles, DEG * count, LANES), jnp.float32),
        pltpu.VMEM((S, LANES), jnp.float32),
    ]


def table_cost(count, points):
    cells = count * points * S
    return pl.CostEstimate(flops=cells * 3 * S * 2, bytes_accessed=cells, transcendentals=cells)


def moments_call(group, count, shared, wd=None, phi=None, dens=None, w=None):
    points = shared[-1].shape[2]
    fresh = wd is None
    out = [jax.ShapeDtypeStruct((count, 3 * S // 2, LANES), jnp.bfloat16)]
    args = list(shared)
    if fresh:
        out.append(jax.ShapeDtypeStruct((3, points), jnp.float32))
        args += [phi, dens, w]
    else:
        args += [wd]
    return pl.pallas_call(
        functools.partial(moments_kernel, group, count, fresh),
        out_shape=out,
        in_specs=[SMEM] * 4 + [VMEM] * (len(args) - 4),
        out_specs=[VMEM] * len(out),
        scratch_shapes=table_scratch(count, points),
        cost_estimate=table_cost(count, points),
        name="moments",
    )(*args)


def field_kernel(groups, size, carried, kept, last, *refs):
    (atoms_ref, pos_ref, blocks_ref, widths_ref, pts_ref), refs = refs[:5], refs[5:]
    tabs, refs = refs[: len(groups)], refs[len(groups) :]
    count = len(groups) * size
    if carried:
        acc_in, refs = refs[0], refs[1:]
    if last:
        (phi_ref, w_ref, marks_ref), outs, refs = refs[:3], refs[3:7], refs[7:]
    else:
        acc_ref, refs = refs[0], refs[1:]
    if kept:
        plane_ref, refs = refs[0], refs[1:]
        for order, tab in enumerate(tabs):
            plane_ref[order ^ lax.axis_index("col")] = tab[lax.axis_index("batch")]
    dist_ref, polar_ref, side_ref, scale_ref = refs[:4]
    if last:
        acc_ref, oper_ref = refs[4:]
    points = pts_ref.shape[2]
    finders = [atom_finder(group, atoms_ref) for group in groups]
    prepare([atom_at(i) for atom_at in finders for i in range(size)], pos_ref, pts_ref, dist_ref, polar_ref, side_ref)
    prepare_shells(widths_ref, scale_ref)
    acc_ref[...] = acc_in[...] if carried else jnp.zeros_like(acc_ref)

    def body(i, carry, tab_ref, atom_at, base):
        k = base + i
        blocks = blocks_ref[atom_at(i)]

        def run(live):
            half = live // 2
            middle, scale = shell_columns(blocks, live, scale_ref)
            table = tab_ref[i].astype(jnp.float32)
            lines = []
            for c in range(3):
                block = table[c * (S // 2) : c * (S // 2) + half]
                lines += [block[:, :S], block[:, S:]]
            left = jnp.concatenate(lines, axis=0).astype(jnp.bfloat16)
            for start in range(0, points, 256):
                t = start // LANES
                right = jnp.concatenate(
                    [angular_tile(k, count, t + d, polar_ref, side_ref) for d in range(2)], axis=1
                )
                spread = jnp.dot(left, right, preferred_element_type=jnp.float32)
                for d in range(2):
                    here = pl.ds(start + d * LANES, LANES)
                    radial = radial_tile(k, t + d, middle, scale, dist_ref)
                    for c in range(3):
                        sums = acc_ref[pl.ds(8 * c, 8), here]
                        for r in range(0, live, 8):
                            at = c * live + r
                            sums += radial[r : r + 8] * spread[at : at + 8, d * LANES : (d + 1) * LANES]
                        acc_ref[pl.ds(8 * c, 8), here] = sums

        by_live(blocks, run)
        return carry

    for order, atom_at in enumerate(finders):
        step = functools.partial(body, tab_ref=tabs[order], atom_at=atom_at, base=order * size)
        lax.fori_loop(0, size, step, 0)
    if last:
        piece = phi_ref.shape[1] // 2
        third = piece // 3
        sides = (lax.axis_index("row"), lax.axis_index("col"))
        halves = [[flip ^ side for flip in range(2)] for side in sides]
        spans = [[pl.ds(pl.multiple_of(h * piece, 32), piece) for h in pair] for pair in halves]
        quads = {}
        for c in range(3):
            for start in range(0, points, 256):
                here = pl.ds(start, 256)
                total = jnp.sum(acc_ref[pl.ds(8 * c, 8), here], axis=0, keepdims=True)
                wide = phi_ref[0, :, here].astype(jnp.float32)
                oper_ref[:, here] = (wide * (w_ref[:, here] * total)).astype(jnp.bfloat16)
            for x in range(2):
                for y in range(2):
                    quads[c, x, y] = lax.dot_general(
                        oper_ref[spans[0][x], :],
                        phi_ref[0, spans[1][y], :],
                        NT,
                        preferred_element_type=jnp.float32,
                    )
        for x in range(2):
            for y in range(2):
                q0, q1, q2 = (quads[c, x, y] for c in range(3))
                marks = [marks_ref[halves[0][x]], marks_ref[halves[1][y]]]
                marks = jnp.concatenate(marks + [jnp.zeros((third - 16, third), jnp.float32)], axis=0)
                parts = [q2[b * third : (b + 1) * third, 2 * third :] for b in range(3)] + [marks]
                blocks = [
                    jnp.concatenate([q0, q2[:, :third]], axis=1),
                    jnp.concatenate([q1, q2[:, third : 2 * third]], axis=1),
                    jnp.concatenate(parts, axis=1),
                ]
                outs[2 * y + x][0] = jnp.concatenate(blocks, axis=0).astype(jnp.bfloat16)


def field_call(groups, size, shared, tables, acc=None, keep=True, ends=None):
    points = shared[-1].shape[2]
    last = ends is not None
    count = len(groups) * size
    args = list(shared) + list(tables) + ([] if acc is None else [acc])
    scratch = table_scratch(count, points)
    if last:
        args += ends
        third = ends[0].shape[1] // 6
        out = [jax.ShapeDtypeStruct((1, 7 * third, LANES), jnp.bfloat16)] * 4
        scratch += [pltpu.VMEM((24, points), jnp.float32), pltpu.VMEM(ends[0].shape[1:], jnp.bfloat16)]
    else:
        out = [jax.ShapeDtypeStruct((24, points), jnp.float32)]
    if keep:
        out.append(jax.ShapeDtypeStruct((len(groups),) + tables[0].shape[1:], jnp.bfloat16))
    return pl.pallas_call(
        functools.partial(field_kernel, groups, size, acc is not None, keep, last),
        out_shape=out,
        in_specs=[SMEM] * 4 + [VMEM] * (len(args) - 4),
        out_specs=[VMEM] * len(out),
        scratch_shapes=scratch,
        cost_estimate=table_cost(count, points),
        name="field",
    )(*args)


def place_kernel(pieces, carried, piece, tile, *refs):
    stacks, refs = refs[:pieces], refs[pieces:]
    if carried:
        acc_in, refs = refs[0], refs[1:]
    out_ref, rows_ref, wide_ref = refs
    third = piece // 3
    group = 4
    total = rows_ref.shape[1] // piece
    lane = lax.broadcasted_iota(jnp.int32, (piece, LANES), 1)
    sub = lax.broadcasted_iota(jnp.int32, (tile, LANES), 0)
    per = total // pieces
    for first in range(0, total, group):
        strips = []
        for g in range(first, first + group):
            ref, at = stacks[g // per], g % per
            tail = ref[at, pl.ds(2 * piece, third), :].astype(jnp.float32)
            marks = tail[: third // 2, 3 * third :]
            row_mark = marks[0:3] * 32.0 + marks[3:6]
            col_mark = marks[8:11] * 32.0 + marks[11:14]
            strips += [row_mark[b : b + 1] for b in range(3)]
            flat = jnp.concatenate([col_mark[b : b + 1] for b in range(3)] + [col_mark[0:1]], axis=1)
            column = jnp.transpose(jnp.broadcast_to(flat, (LANES, LANES)))[:piece].astype(jnp.int32)
            hits = jnp.concatenate(
                [
                    (column == lane + u).astype(jnp.float32).astype(jnp.bfloat16)
                    for u in range(0, tile, LANES)
                ],
                axis=1,
            )
            upper = ref[at, pl.ds(0, piece), :].astype(jnp.float32)
            lower = ref[at, pl.ds(piece, piece), :].astype(jnp.float32)
            rest = jnp.concatenate([tail[:, b * third : (b + 1) * third] for b in range(3)], axis=0)
            shared = jnp.concatenate([upper[:, piece:], lower[:, piece:], rest], axis=1)
            quads = jnp.concatenate([upper[:, :piece], lower[:, :piece], shared], axis=0)
            spread = jnp.dot(
                quads.astype(jnp.bfloat16), hits, preferred_element_type=jnp.float32
            ).astype(jnp.bfloat16)
            for c in range(3):
                wide_ref[c, pl.ds(g * piece, piece), :] = spread[c * piece : (c + 1) * piece]
        strip = jnp.concatenate(strips, axis=1).astype(jnp.int32)
        for start in range(0, group * piece, LANES):
            rows_ref[:, pl.ds(first * piece + start, LANES)] = (
                (sub == strip[:, start : start + LANES]).astype(jnp.float32).astype(jnp.bfloat16)
            )

    step = 256

    def body(i, carry):
        c, t = i // (tile // step), (i % (tile // step)) * step
        here = pl.ds(pl.multiple_of(t, step), step)
        value = jnp.dot(rows_ref[here, :], wide_ref[c], preferred_element_type=jnp.float32)
        if carried:
            value += acc_in[c, here, :]
        out_ref[c, here, :] = value.astype(out_ref.dtype)
        return carry

    lax.fori_loop(0, 3 * (tile // step), body, 0)


def place_call(stacks, piece, tile, acc=None, final=True):
    total = sum(stack.shape[0] for stack in stacks)
    depth = total * piece
    args = list(stacks) + ([] if acc is None else [acc])
    return pl.pallas_call(
        functools.partial(place_kernel, len(stacks), acc is not None, piece, tile),
        out_shape=jax.ShapeDtypeStruct((3, tile, tile), jnp.bfloat16 if final else jnp.float32),
        in_specs=[VMEM] * len(args),
        out_specs=VMEM,
        scratch_shapes=[
            pltpu.VMEM((tile, depth), jnp.bfloat16),
            pltpu.VMEM((3, depth, tile), jnp.bfloat16),
        ],
        input_output_aliases={} if acc is None or final else {len(stacks): 0},
        compiler_params=pltpu.CompilerParams(vmem_limit_bytes=28 << 20),
        cost_estimate=pl.CostEstimate(
            flops=8 * 3 * depth * tile * tile, bytes_accessed=12 * tile * tile, transcendentals=0
        ),
        name="place",
    )(*args)


def apply_green(charges, kernels):
    shaped = charges.astype(jnp.bfloat16).reshape(-1, 3, S, DEG, DEG)
    kernel_rows = kernels.reshape(-1, DEG, S, S)
    result = jnp.einsum(
        "xast,xctam->xcsam", kernel_rows, shaped, preferred_element_type=jnp.float32
    )
    return result.astype(jnp.bfloat16).reshape(-1, 3 * S * DEG * DEG)


def swap(value, axis, mask=1):
    size = lax.axis_size(axis)
    return lax.ppermute(value, axis, [(i, i ^ mask) for i in range(size)])


def on_device(
    basis_values,
    density_matrix,
    points,
    weights,
    intersection,
    basis_index,
    atom_positions,
    shell_blocks,
    shell_widths,
    green,
):
    atoms = intersection[0]
    labels = basis_index[0]
    owners = lax.axis_size("batch")
    parts = lax.axis_size("row")
    sides = lax.axis_size("col")
    row, col = lax.axis_index("row"), lax.axis_index("col")
    count = atoms.shape[0]
    slots = (count + owners - 1) // owners
    holding = green.shape[0]
    every_atom = atom_positions.shape[1]
    width = 3 * S * DEG * DEG
    lines = width // LANES
    highest = lax.Precision.HIGHEST
    dense = count == every_atom and holding == parts * sides
    plane = ("row", "col")
    across = [(i, i ^ 3) for i in range(parts * sides)]
    half, group = count // 2, count // 4
    shared = (atoms, atom_positions, shell_blocks, shell_widths, points)
    wanted = ((sides, None, 0), (sides, None, 1)) if dense else (0, half)
    listed = [(holding, f & 1, f >> 1) if dense else f * group for f in range(4)]
    other, weighted = moments_call(
        wanted[1], half, shared, phi=basis_values, dens=density_matrix, w=weights
    )
    mate = swap(other, "col") if dense else other
    first = moments_call(wanted[0], half, shared, wd=weighted)[0]
    if dense:
        held = first + mate
        shares = lax.all_to_all(held, ("batch", "row"), split_axis=0, concat_axis=0, tiled=True)
        charges = jnp.sum(shares.astype(jnp.float32), axis=0)
        kernels = lax.dynamic_index_in_dim(green, row * sides + col, 0, keepdims=True)
        mine = apply_green(charges.reshape(1, width), kernels).reshape(1, lines, LANES)
        own = lax.all_to_all(
            jnp.broadcast_to(mine, (owners, lines, LANES)),
            "batch",
            split_axis=0,
            concat_axis=0,
            tiled=True,
        )
        beside = swap(own, "row")
        beyond = lax.ppermute(own, plane, across)
        tables = [own, beside, swap(own, "col"), beyond]
    else:
        moments = jnp.concatenate([first, other])
        moments = moments.astype(jnp.float32).reshape(count, width)
        home = atoms // holding
        local_slot = atoms % holding
        order = jnp.arange(count)
        before = (home[None, :] == home[:, None]) & (order[None, :] < order[:, None])
        place = home * slots + jnp.sum(before, axis=1)
        routing = jnp.arange(owners * slots)[:, None] == place[None, :]
        outgoing = jnp.dot(routing.astype(jnp.float32), moments, precision=highest).reshape(
            owners, slots, width
        )
        tags = (jnp.sum(jnp.where(routing, local_slot[None, :] + 1, 0), axis=1) - 1).reshape(
            owners, slots
        )
        incoming, sources = (
            lax.all_to_all(outgoing, "batch", split_axis=0, concat_axis=0, tiled=True),
            lax.all_to_all(tags, "batch", split_axis=0, concat_axis=0, tiled=True),
        )
        collect = jnp.arange(holding)[:, None] == sources.reshape(1, owners * slots)
        partial_value = jnp.dot(
            collect.astype(jnp.float32), incoming.reshape(owners * slots, width), precision=highest
        )
        totals = lax.psum(partial_value, ("row", "col"))
        potential = apply_green(totals, green)
        back = jnp.dot(
            collect.T.astype(jnp.bfloat16), potential, preferred_element_type=jnp.float32
        ).astype(jnp.bfloat16)
        returned = lax.all_to_all(
            back.reshape(owners, slots, width), "batch", split_axis=0, concat_axis=0, tiled=True
        )
        table = jnp.dot(
            routing.T.astype(jnp.bfloat16),
            returned.reshape(owners * slots, width),
            preferred_element_type=jnp.float32,
        )
        table = table.astype(jnp.bfloat16).reshape(count, lines, LANES)
        tables = [table[place * group : (place + 1) * group] for place in range(4)]
    piece = labels.shape[0] // parts
    tile = NB // parts
    inner = labels.reshape(parts, 3, piece // 3) - jnp.arange(parts)[:, None, None] * tile
    marks = jnp.concatenate([inner // 32, inner % 32, inner[:, :2] * 0], axis=1)
    marks = marks.astype(jnp.float32)
    ends = [basis_values, weights, marks]
    spread = functools.partial(field_call, size=group, shared=shared, keep=dense)
    field, *ours = spread((listed[0], listed[2]), tables=[tables[0], tables[2]])
    load = spread((listed[1], listed[3]), tables=[tables[1], tables[3]], acc=field, ends=ends)
    if dense:
        ours, theirs = ours[0], load[4]
        potential = jnp.concatenate(
            [jnp.where(row == 0, ours, theirs), jnp.where(row == 0, theirs, ours)]
        ).reshape(holding, width)
    got = [swap(load[2], "col"), swap(load[1], "row"), lax.ppermute(load[3], plane, across)]
    plane_load = jnp.concatenate([load[0]] + got, axis=0)
    if owners <= 8:
        near, far = [plane_load], []
        for step in range(2, owners, 2):
            near.append(swap(plane_load, "batch", step))
        for line in near:
            far.append(swap(line, "batch"))
        stages = [near[:1], far[:1] + near[1:2], far[1:2], near[2:], far[2:]]
        stages = [lines for lines in stages if lines]
        total = None
        for order, lines in enumerate(stages):
            total = place_call(lines, piece, tile, total, final=lines is stages[-1])
        hamiltonian = total
    else:
        everyone = lax.all_gather(plane_load, "batch", axis=0)
        chunk = 4
        everyone = everyone.reshape((owners // chunk, chunk * 4) + plane_load.shape[1:])

        def add(total, item):
            return place_call([item], piece, tile, total, final=False), None

        total, _ = lax.scan(add, jnp.zeros((3, tile, tile), jnp.float32), everyone)
        hamiltonian = total.astype(jnp.bfloat16)
    return (potential, hamiltonian)


def solution(mesh):
    return jax.shard_map(
        on_device,
        mesh=mesh,
        in_specs=(
            P(("batch", "row", "col"), None, None),
            P(("batch", "row", "col"), None, None, None),
            P(("batch", "row", "col"), None, None),
            P(("batch", "row", "col"), None),
            P(("batch", "row", "col"), None),
            P(("batch", "row", "col"), None),
            P(),
            P(),
            P(),
            P("batch", None, None),
        ),
        out_specs=(P("batch", None), P(None, "row", "col")),
        check_vma=False,
    )
```

```python
import functools

import jax
import jax.numpy as jnp
from jax import lax
from jax.experimental import pallas as pl
from jax.experimental.pallas import tpu as pltpu
from jax.sharding import PartitionSpec as P


S = 64
DEG = 8
NB = 1536
LANES = 128
FAR = 1.0e6
LOG2E = 1.4426950408889634
NT = (((1,), (1,)), ((), ()))
SMEM = pl.BlockSpec(memory_space=pltpu.SMEM)
VMEM = pl.BlockSpec(memory_space=pltpu.VMEM)


def atom_finder(group, atoms_ref):
    if isinstance(group, int):
        return lambda i: atoms_ref[group + i]
    stride, row_flip, col_flip = group
    base = lax.axis_index("col") ^ col_flip
    if row_flip is not None:
        base = base + (lax.axis_index("row") ^ row_flip) * 2
    return lambda i: base + i * stride


def prepare(chosen, pos_ref, pts_ref, dist_ref, polar_ref, side_ref):
    count = len(chosen)
    rows = lax.broadcasted_iota(jnp.int32, (count, LANES), 0)
    centre = []
    for axis in range(3):
        column = jnp.zeros((count, LANES), jnp.float32)
        for k, atom in enumerate(chosen):
            column = jnp.where(rows == k, pos_ref[axis, atom], column)
        centre.append(column)
    for t in range(pts_ref.shape[2] // LANES):
        here = pl.ds(t * LANES, LANES)
        delta = [pts_ref[0, pl.ds(axis, 1), here] - centre[axis] for axis in range(3)]
        square = delta[0] * delta[0] + delta[1] * delta[1] + delta[2] * delta[2] + 0.01
        inverse = lax.rsqrt(square)
        dist_ref[t] = square * inverse
        for ladder, u in ((polar_ref, delta[2] * inverse), (side_ref, delta[0] * inverse)):
            older, old = jnp.ones_like(u), u
            ladder[t, pl.ds(0, count), :] = older
            ladder[t, pl.ds(count, count), :] = old
            for order in range(2, DEG):
                older, old = old, 2.0 * u * old - older
                ladder[t, pl.ds(order * count, count), :] = old


def prepare_shells(widths_ref, scale_ref):
    rows = lax.broadcasted_iota(jnp.int32, (8, LANES), 0)
    for start in range(0, S, 8):
        column = jnp.zeros((8, LANES), jnp.float32)
        for j in range(8):
            place = start + j
            shell = 2 * place if place < S // 2 else 2 * place - (S - 1)
            column = jnp.where(rows == j, widths_ref[shell], column)
        scale_ref[pl.ds(start, 8), :] = -LOG2E / (column * column)


def shell_columns(blocks, live, scale_ref):
    half = live // 2
    place = lax.broadcasted_iota(jnp.int32, (live, LANES), 0)
    shell = jnp.where(place < half, 2 * place, 2 * place - (live - 1))
    middle = jnp.where(shell < 8 * blocks, shell.astype(jnp.float32) * (4.0 / S), FAR)
    scale = jnp.concatenate(
        [scale_ref[pl.ds(0, half), :], scale_ref[pl.ds(S // 2, half), :]], axis=0
    )
    return middle, scale


def angular_tile(k, count, t, polar_ref, side_ref):
    side = side_ref[t, pl.ds(k, DEG, stride=count), :]
    return jnp.concatenate(
        [
            polar_ref[t, pl.ds(order * count + k, DEG, stride=0), :] * side
            for order in range(DEG)
        ],
        axis=0,
    ).astype(jnp.bfloat16)


def radial_tile(k, t, middle, scale, dist_ref):
    dist = dist_ref[t, pl.ds(k, 8, stride=0), :]
    gap = jnp.concatenate([dist] * (middle.shape[0] // 8), axis=0) - middle
    return jnp.exp2(gap * (gap * scale))


def moments_kernel(group, count, fresh, *refs):
    if fresh:
        (
            atoms_ref, pos_ref, blocks_ref, widths_ref, pts_ref, phi_ref, dens_ref, w_ref,
            out_ref, wd_ref, dist_ref, polar_ref, side_ref, scale_ref,
        ) = refs
    else:
        (
            atoms_ref, pos_ref, blocks_ref, widths_ref, pts_ref, wd_ref,
            out_ref, dist_ref, polar_ref, side_ref, scale_ref,
        ) = refs
    points = pts_ref.shape[2]
    if fresh:
        for start in range(0, points, 256):
            here = pl.ds(start, 256)
            phi = phi_ref[0, :, here]
            wide = phi.astype(jnp.float32)
            for c in range(3):
                product = jnp.dot(dens_ref[0, c], phi, preferred_element_type=jnp.float32)
                density = jnp.sum(wide * product, axis=0, keepdims=True)
                wd_ref[pl.ds(c, 1), here] = w_ref[:, here] * density
    atom_at = atom_finder(group, atoms_ref)
    prepare([atom_at(i) for i in range(count)], pos_ref, pts_ref, dist_ref, polar_ref, side_ref)
    prepare_shells(widths_ref, scale_ref)

    def body(k, carry):
        blocks = blocks_ref[atom_at(k)]

        live = S
        middle, scale = shell_columns(blocks, live, scale_ref)
        total = jnp.zeros((3 * live, S), jnp.float32)
        for start in range(0, points, 256):
            scaled, angles = [[], [], []], []
            for inner in (start, start + LANES):
                t = inner // LANES
                radial = radial_tile(k, t, middle, scale, dist_ref).astype(jnp.bfloat16)
                angles.append(angular_tile(k, count, t, polar_ref, side_ref))
                for c in range(3):
                    row = jnp.broadcast_to(wd_ref[pl.ds(c, 1), pl.ds(inner, LANES)], (16, LANES))
                    row = jnp.concatenate([row.astype(jnp.bfloat16)] * (live // 16), axis=0)
                    scaled[c].append(radial * row)
            left = jnp.concatenate([jnp.concatenate(s, axis=1) for s in scaled], axis=0)
            right = jnp.concatenate(angles, axis=1)
            total += lax.dot_general(left, right, NT, preferred_element_type=jnp.float32)
        half = live // 2
        for c in range(3):
            even = total[c * live : c * live + half]
            odd = total[c * live + half : (c + 1) * live]
            block = jnp.concatenate([even, odd], axis=1)
            if live < S:
                rest = jnp.zeros((S // 2 - half, LANES), jnp.float32)
                block = jnp.concatenate([block, rest], axis=0)
            out_ref[k, pl.ds(c * (S // 2), S // 2), :] = block.astype(out_ref.dtype)

        return carry

    lax.fori_loop(0, count, body, 0, unroll=8)


def table_scratch(count, points):
    tiles = points // LANES
    return [
        pltpu.VMEM((tiles, count, LANES), jnp.float32),
        pltpu.VMEM((tiles, DEG * count, LANES), jnp.float32),
        pltpu.VMEM((tiles, DEG * count, LANES), jnp.float32),
        pltpu.VMEM((S, LANES), jnp.float32),
    ]


def table_cost(count, points):
    cells = count * points * S
    return pl.CostEstimate(flops=cells * 3 * S * 2, bytes_accessed=cells, transcendentals=cells)


def moments_call(group, count, shared, wd=None, phi=None, dens=None, w=None):
    points = shared[-1].shape[2]
    fresh = wd is None
    out = [jax.ShapeDtypeStruct((count, 3 * S // 2, LANES), jnp.bfloat16)]
    args = list(shared)
    if fresh:
        out.append(jax.ShapeDtypeStruct((3, points), jnp.float32))
        args += [phi, dens, w]
    else:
        args += [wd]
    return pl.pallas_call(
        functools.partial(moments_kernel, group, count, fresh),
        out_shape=out,
        in_specs=[SMEM] * 4 + [VMEM] * (len(args) - 4),
        out_specs=[VMEM] * len(out),
        scratch_shapes=table_scratch(count, points),
        cost_estimate=table_cost(count, points),
        name="moments",
    )(*args)


def field_kernel(groups, size, carried, kept, last, *refs):
    (atoms_ref, pos_ref, blocks_ref, widths_ref, pts_ref), refs = refs[:5], refs[5:]
    tabs, refs = refs[: len(groups)], refs[len(groups) :]
    count = len(groups) * size
    if carried:
        acc_in, refs = refs[0], refs[1:]
    if last:
        (phi_ref, w_ref, marks_ref), outs, refs = refs[:3], refs[3:7], refs[7:]
    else:
        acc_ref, refs = refs[0], refs[1:]
    if kept:
        plane_ref, refs = refs[0], refs[1:]
        for order, tab in enumerate(tabs):
            plane_ref[order ^ lax.axis_index("col")] = tab[lax.axis_index("batch")]
    dist_ref, polar_ref, side_ref, scale_ref = refs[:4]
    if last:
        acc_ref, oper_ref = refs[4:]
    points = pts_ref.shape[2]
    finders = [atom_finder(group, atoms_ref) for group in groups]
    prepare([atom_at(i) for atom_at in finders for i in range(size)], pos_ref, pts_ref, dist_ref, polar_ref, side_ref)
    prepare_shells(widths_ref, scale_ref)
    acc_ref[...] = acc_in[...] if carried else jnp.zeros_like(acc_ref)

    def body(i, carry, tab_ref, atom_at, base):
        k = base + i
        blocks = blocks_ref[atom_at(i)]

        live, half = S, S // 2
        middle, scale = shell_columns(blocks, live, scale_ref)
        table = tab_ref[i].astype(jnp.float32)
        lines = []
        for c in range(3):
            block = table[c * (S // 2) : c * (S // 2) + half]
            lines += [block[:, :S], block[:, S:]]
        left = jnp.concatenate(lines, axis=0).astype(jnp.bfloat16)
        for start in range(0, points, 256):
            t = start // LANES
            right = jnp.concatenate(
                [angular_tile(k, count, t + d, polar_ref, side_ref) for d in range(2)], axis=1
            )
            spread = jnp.dot(left, right, preferred_element_type=jnp.float32)
            for d in range(2):
                here = pl.ds(start + d * LANES, LANES)
                radial = radial_tile(k, t + d, middle, scale, dist_ref)
                for c in range(3):
                    sums = acc_ref[pl.ds(8 * c, 8), here]
                    for r in range(0, live, 8):
                        at = c * live + r
                        sums += radial[r : r + 8] * spread[at : at + 8, d * LANES : (d + 1) * LANES]
                    acc_ref[pl.ds(8 * c, 8), here] = sums

        return carry

    for order, atom_at in enumerate(finders):
        step = functools.partial(body, tab_ref=tabs[order], atom_at=atom_at, base=order * size)
        lax.fori_loop(0, size, step, 0, unroll=4)
    if last:
        piece = phi_ref.shape[1] // 2
        third = piece // 3
        sides = (lax.axis_index("row"), lax.axis_index("col"))
        halves = [[flip ^ side for flip in range(2)] for side in sides]
        spans = [[pl.ds(pl.multiple_of(h * piece, 32), piece) for h in pair] for pair in halves]
        quads = {}
        for c in range(3):
            for start in range(0, points, 256):
                here = pl.ds(start, 256)
                total = jnp.sum(acc_ref[pl.ds(8 * c, 8), here], axis=0, keepdims=True)
                wide = phi_ref[0, :, here].astype(jnp.float32)
                oper_ref[:, here] = (wide * (w_ref[:, here] * total)).astype(jnp.bfloat16)
            for x in range(2):
                for y in range(2):
                    quads[c, x, y] = lax.dot_general(
                        oper_ref[spans[0][x], :],
                        phi_ref[0, spans[1][y], :],
                        NT,
                        preferred_element_type=jnp.float32,
                    )
        for x in range(2):
            for y in range(2):
                q0, q1, q2 = (quads[c, x, y] for c in range(3))
                marks = [marks_ref[halves[0][x]], marks_ref[halves[1][y]]]
                marks = jnp.concatenate(marks + [jnp.zeros((third - 16, third), jnp.float32)], axis=0)
                parts = [q2[b * third : (b + 1) * third, 2 * third :] for b in range(3)] + [marks]
                blocks = [
                    jnp.concatenate([q0, q2[:, :third]], axis=1),
                    jnp.concatenate([q1, q2[:, third : 2 * third]], axis=1),
                    jnp.concatenate(parts, axis=1),
                ]
                outs[2 * y + x][0] = jnp.concatenate(blocks, axis=0).astype(jnp.bfloat16)


def field_call(groups, size, shared, tables, acc=None, keep=True, ends=None):
    points = shared[-1].shape[2]
    last = ends is not None
    count = len(groups) * size
    args = list(shared) + list(tables) + ([] if acc is None else [acc])
    scratch = table_scratch(count, points)
    if last:
        args += ends
        third = ends[0].shape[1] // 6
        out = [jax.ShapeDtypeStruct((1, 7 * third, LANES), jnp.bfloat16)] * 4
        scratch += [pltpu.VMEM((24, points), jnp.float32), pltpu.VMEM(ends[0].shape[1:], jnp.bfloat16)]
    else:
        out = [jax.ShapeDtypeStruct((24, points), jnp.float32)]
    if keep:
        out.append(jax.ShapeDtypeStruct((len(groups),) + tables[0].shape[1:], jnp.bfloat16))
    return pl.pallas_call(
        functools.partial(field_kernel, groups, size, acc is not None, keep, last),
        out_shape=out,
        in_specs=[SMEM] * 4 + [VMEM] * (len(args) - 4),
        out_specs=[VMEM] * len(out),
        scratch_shapes=scratch,
        cost_estimate=table_cost(count, points),
        name="field",
    )(*args)


def place_kernel(pieces, carried, final, piece, tile, *refs):
    stacks, refs = refs[:pieces], refs[pieces:]
    if carried:
        acc_in, refs = refs[0], refs[1:]
    out_ref, rows_ref, wide_ref = refs[:3]
    if final:
        hold_ref, sem_ref = refs[3:]
    third = piece // 3
    group = 4
    total = rows_ref.shape[1] // piece
    lane = lax.broadcasted_iota(jnp.int32, (piece, LANES), 1).astype(jnp.int16)
    sub = lax.broadcasted_iota(jnp.int32, (tile, LANES), 0).astype(jnp.int16)
    one, zero = jnp.bfloat16(1), jnp.bfloat16(0)
    per = total // pieces
    for first in range(0, total, group):
        strips = []
        for g in range(first, first + group):
            ref, at = stacks[g // per], g % per
            tail = ref[at, pl.ds(2 * piece, third), :].astype(jnp.float32)
            marks = tail[: third // 2, 3 * third :]
            row_mark = marks[0:3] * 32.0 + marks[3:6]
            col_mark = marks[8:11] * 32.0 + marks[11:14]
            strips += [row_mark[b : b + 1] for b in range(3)]
            flat = jnp.concatenate([col_mark[b : b + 1] for b in range(3)] + [col_mark[0:1]], axis=1)
            column = jnp.transpose(jnp.broadcast_to(flat, (LANES, LANES)))[:piece].astype(jnp.int32).astype(jnp.int16)
            hits = jnp.concatenate(
                [
                    jnp.where(column == lane + u, one, zero)
                    for u in range(0, tile, LANES)
                ],
                axis=1,
            )
            upper = ref[at, pl.ds(0, piece), :].astype(jnp.float32)
            lower = ref[at, pl.ds(piece, piece), :].astype(jnp.float32)
            rest = jnp.concatenate([tail[:, b * third : (b + 1) * third] for b in range(3)], axis=0)
            shared = jnp.concatenate([upper[:, piece:], lower[:, piece:], rest], axis=1)
            quads = jnp.concatenate([upper[:, :piece], lower[:, :piece], shared], axis=0)
            spread = jnp.dot(
                quads.astype(jnp.bfloat16), hits, preferred_element_type=jnp.float32
            ).astype(jnp.bfloat16)
            for c in range(3):
                wide_ref[c, pl.ds(g * piece, piece), :] = spread[c * piece : (c + 1) * piece]
        strip = jnp.concatenate(strips, axis=1).astype(jnp.int32)
        strip = jnp.broadcast_to(strip, (16, strip.shape[1])).astype(jnp.int16)
        strip = jnp.concatenate([strip] * (tile // 16), axis=0)
        for start in range(0, group * piece, LANES):
            rows_ref[:, pl.ds(first * piece + start, LANES)] = (
                jnp.where(sub == strip[:, start : start + LANES], one, zero)
            )

    copies = []
    for c in range(3):
        value = jnp.dot(rows_ref[...], wide_ref[c], preferred_element_type=jnp.float32)
        if carried:
            value += acc_in[c]
        if final:
            hold_ref[c] = value.astype(out_ref.dtype)
            copies.append(pltpu.make_async_copy(hold_ref.at[c], out_ref.at[c], sem_ref.at[c]))
            copies[-1].start()
        else:
            out_ref[c] = value
    for copy in copies:
        copy.wait()


def place_call(stacks, piece, tile, acc=None, final=True):
    total = sum(stack.shape[0] for stack in stacks)
    depth = total * piece
    args = list(stacks) + ([] if acc is None else [acc])
    return pl.pallas_call(
        functools.partial(place_kernel, len(stacks), acc is not None, final, piece, tile),
        out_shape=jax.ShapeDtypeStruct((3, tile, tile), jnp.bfloat16 if final else jnp.float32),
        in_specs=[VMEM] * len(args),
        out_specs=pl.BlockSpec(memory_space=pl.ANY) if final else VMEM,
        scratch_shapes=[
            pltpu.VMEM((tile, depth), jnp.bfloat16),
            pltpu.VMEM((3, depth, tile), jnp.bfloat16),
        ]
        + ([pltpu.VMEM((3, tile, tile), jnp.bfloat16), pltpu.SemaphoreType.DMA((3,))] if final else []),
        input_output_aliases={} if acc is None or final else {len(stacks): 0},
        compiler_params=pltpu.CompilerParams(vmem_limit_bytes=28 << 20),
        cost_estimate=pl.CostEstimate(
            flops=8 * 3 * depth * tile * tile, bytes_accessed=12 * tile * tile, transcendentals=0
        ),
        name="place",
    )(*args)


def apply_green(charges, kernels):
    shaped = charges.astype(jnp.bfloat16).reshape(-1, 3, S, DEG, DEG)
    kernel_rows = kernels.reshape(-1, DEG, S, S)
    result = jnp.einsum(
        "xast,xctam->xcsam", kernel_rows, shaped, preferred_element_type=jnp.float32
    )
    return result.astype(jnp.bfloat16).reshape(-1, 3 * S * DEG * DEG)


def swap(value, axis, mask=1):
    size = lax.axis_size(axis)
    return lax.ppermute(value, axis, [(i, i ^ mask) for i in range(size)])


def on_device(
    basis_values,
    density_matrix,
    points,
    weights,
    intersection,
    basis_index,
    atom_positions,
    shell_blocks,
    shell_widths,
    green,
):
    atoms = intersection[0]
    labels = basis_index[0]
    owners = lax.axis_size("batch")
    parts = lax.axis_size("row")
    sides = lax.axis_size("col")
    row, col = lax.axis_index("row"), lax.axis_index("col")
    count = atoms.shape[0]
    slots = (count + owners - 1) // owners
    holding = green.shape[0]
    every_atom = atom_positions.shape[1]
    width = 3 * S * DEG * DEG
    lines = width // LANES
    highest = lax.Precision.HIGHEST
    dense = count == every_atom and holding == parts * sides
    plane = ("row", "col")
    across = [(i, i ^ 3) for i in range(parts * sides)]
    half, group = count // 2, count // 4
    shared = (atoms, atom_positions, shell_blocks, shell_widths, points)
    wanted = ((sides, None, 0), (sides, None, 1)) if dense else (0, half)
    listed = [(holding, f & 1, f >> 1) if dense else f * group for f in range(4)]
    other, weighted = moments_call(
        wanted[1], half, shared, phi=basis_values, dens=density_matrix, w=weights
    )
    mate = swap(other, "col") if dense else other
    first = moments_call(wanted[0], half, shared, wd=weighted)[0]
    if dense:
        held = first + mate
        shares = lax.all_to_all(held, ("batch", "row"), split_axis=0, concat_axis=0, tiled=True)
        charges = jnp.sum(shares.astype(jnp.float32), axis=0)
        kernels = lax.dynamic_index_in_dim(green, row * sides + col, 0, keepdims=True)
        mine = apply_green(charges.reshape(1, width), kernels).reshape(1, lines, LANES)
        own = lax.all_to_all(
            jnp.broadcast_to(mine, (owners, lines, LANES)),
            "batch",
            split_axis=0,
            concat_axis=0,
            tiled=True,
        )
        beside = swap(own, "row")
        beyond = lax.ppermute(own, plane, across)
        tables = [own, beside, swap(own, "col"), beyond]
    else:
        moments = jnp.concatenate([first, other])
        moments = moments.astype(jnp.float32).reshape(count, width)
        home = atoms // holding
        local_slot = atoms % holding
        order = jnp.arange(count)
        before = (home[None, :] == home[:, None]) & (order[None, :] < order[:, None])
        place = home * slots + jnp.sum(before, axis=1)
        routing = jnp.arange(owners * slots)[:, None] == place[None, :]
        outgoing = jnp.dot(routing.astype(jnp.float32), moments, precision=highest).reshape(
            owners, slots, width
        )
        tags = (jnp.sum(jnp.where(routing, local_slot[None, :] + 1, 0), axis=1) - 1).reshape(
            owners, slots
        )
        incoming, sources = (
            lax.all_to_all(outgoing, "batch", split_axis=0, concat_axis=0, tiled=True),
            lax.all_to_all(tags, "batch", split_axis=0, concat_axis=0, tiled=True),
        )
        collect = jnp.arange(holding)[:, None] == sources.reshape(1, owners * slots)
        partial_value = jnp.dot(
            collect.astype(jnp.float32), incoming.reshape(owners * slots, width), precision=highest
        )
        totals = lax.psum(partial_value, ("row", "col"))
        potential = apply_green(totals, green)
        back = jnp.dot(
            collect.T.astype(jnp.bfloat16), potential, preferred_element_type=jnp.float32
        ).astype(jnp.bfloat16)
        returned = lax.all_to_all(
            back.reshape(owners, slots, width), "batch", split_axis=0, concat_axis=0, tiled=True
        )
        table = jnp.dot(
            routing.T.astype(jnp.bfloat16),
            returned.reshape(owners * slots, width),
            preferred_element_type=jnp.float32,
        )
        table = table.astype(jnp.bfloat16).reshape(count, lines, LANES)
        tables = [table[place * group : (place + 1) * group] for place in range(4)]
    piece = labels.shape[0] // parts
    tile = NB // parts
    inner = labels.reshape(parts, 3, piece // 3) - jnp.arange(parts)[:, None, None] * tile
    marks = jnp.concatenate([inner // 32, inner % 32, inner[:, :2] * 0], axis=1)
    marks = marks.astype(jnp.float32)
    ends = [basis_values, weights, marks]
    spread = functools.partial(field_call, size=group, shared=shared, keep=dense)
    field, *ours = spread((listed[0], listed[2]), tables=[tables[0], tables[2]])
    load = spread((listed[1], listed[3]), tables=[tables[1], tables[3]], acc=field, ends=ends)
    if dense:
        ours, theirs = ours[0], load[4]
        potential = jnp.concatenate(
            [jnp.where(row == 0, ours, theirs), jnp.where(row == 0, theirs, ours)]
        ).reshape(holding, width)
    got = [swap(load[2], "col"), swap(load[1], "row"), lax.ppermute(load[3], plane, across)]
    plane_load = jnp.concatenate([load[0]] + got, axis=0)
    if owners <= 8:
        near, far = [plane_load], []
        for step in range(2, owners, 2):
            near.append(swap(plane_load, "batch", step))
        for line in near:
            far.append(swap(line, "batch"))
        stages = [near[:1]] + [list(pair) for pair in zip(near[1:], far)] + [far[-1:]]
        total = None
        for order, lines in enumerate(stages):
            total = place_call(lines, piece, tile, total, final=lines is stages[-1])
        hamiltonian = total
    else:
        everyone = lax.all_gather(plane_load, "batch", axis=0)
        chunk = 2
        everyone = everyone.reshape((owners // chunk, chunk * 4) + plane_load.shape[1:])

        def add(total, item):
            return place_call([item], piece, tile, total, final=False), None

        total, _ = lax.scan(add, jnp.zeros((3, tile, tile), jnp.float32), everyone)
        hamiltonian = total.astype(jnp.bfloat16)
    return (potential, hamiltonian)


def solution(mesh):
    return jax.shard_map(
        on_device,
        mesh=mesh,
        in_specs=(
            P(("batch", "row", "col"), None, None),
            P(("batch", "row", "col"), None, None, None),
            P(("batch", "row", "col"), None, None),
            P(("batch", "row", "col"), None),
            P(("batch", "row", "col"), None),
            P(("batch", "row", "col"), None),
            P(),
            P(),
            P(),
            P("batch", None, None),
        ),
        out_specs=(P("batch", None), P(None, "row", "col")),
        check_vma=False,
    )
```

```python
import functools

import jax
import jax.numpy as jnp
from jax import lax
from jax.experimental import pallas as pl
from jax.experimental.pallas import tpu as pltpu
from jax.sharding import PartitionSpec as P


S = 64
DEG = 8
NB = 1536
LANES = 128
FAR = 1.0e6
LOG2E = 1.4426950408889634
NT = (((1,), (1,)), ((), ()))
SMEM = pl.BlockSpec(memory_space=pltpu.SMEM)
VMEM = pl.BlockSpec(memory_space=pltpu.VMEM)


def atom_finder(group, atoms_ref):
    if isinstance(group, int):
        return lambda i: atoms_ref[group + i]
    stride, row_flip, col_flip = group
    base = lax.axis_index("col") ^ col_flip
    if row_flip is not None:
        base = base + (lax.axis_index("row") ^ row_flip) * 2
    return lambda i: base + i * stride


def prepare(chosen, pos_ref, pts_ref, dist_ref, polar_ref, side_ref):
    count = len(chosen)
    rows = lax.broadcasted_iota(jnp.int32, (count, LANES), 0)
    centre = []
    for axis in range(3):
        column = jnp.zeros((count, LANES), jnp.float32)
        for k, atom in enumerate(chosen):
            column = jnp.where(rows == k, pos_ref[axis, atom], column)
        centre.append(column)
    for t in range(pts_ref.shape[2] // LANES):
        here = pl.ds(t * LANES, LANES)
        delta = [pts_ref[axis, :, here] - centre[axis] for axis in range(3)]
        square = delta[0] * delta[0] + delta[1] * delta[1] + delta[2] * delta[2] + 0.01
        inverse = lax.rsqrt(square)
        dist_ref[t] = square * inverse
        for ladder, u in ((polar_ref, delta[2] * inverse), (side_ref, delta[0] * inverse)):
            older, old = jnp.ones_like(u), u
            ladder[t, pl.ds(0, count), :] = older
            ladder[t, pl.ds(count, count), :] = old
            for order in range(2, DEG):
                older, old = old, 2.0 * u * old - older
                ladder[t, pl.ds(order * count, count), :] = old


def prepare_shells(widths_ref, scale_ref):
    rows = lax.broadcasted_iota(jnp.int32, (8, LANES), 0)
    for start in range(0, S, 8):
        column = jnp.zeros((8, LANES), jnp.float32)
        for j in range(8):
            place = start + j
            shell = 2 * place if place < S // 2 else 2 * place - (S - 1)
            column = jnp.where(rows == j, widths_ref[shell], column)
        scale_ref[pl.ds(start, 8), :] = -LOG2E / (column * column)


def shell_columns(blocks, live, scale_ref):
    half = live // 2
    place = lax.broadcasted_iota(jnp.int32, (live, LANES), 0)
    shell = jnp.where(place < half, 2 * place, 2 * place - (live - 1))
    middle = jnp.where(shell < 8 * blocks, shell.astype(jnp.float32) * (4.0 / S), FAR)
    scale = jnp.concatenate(
        [scale_ref[pl.ds(0, half), :], scale_ref[pl.ds(S // 2, half), :]], axis=0
    )
    return middle, scale


def angular_tile(k, count, t, polar_ref, side_ref):
    side = side_ref[t, pl.ds(k, DEG, stride=count), :]
    return jnp.concatenate(
        [
            polar_ref[t, pl.ds(order * count + k, DEG, stride=0), :] * side
            for order in range(DEG)
        ],
        axis=0,
    ).astype(jnp.bfloat16)


def radial_tile(k, t, middle, scale, dist_ref):
    dist = dist_ref[t, pl.ds(k, 8, stride=0), :]
    gap = jnp.concatenate([dist] * (middle.shape[0] // 8), axis=0) - middle
    return jnp.exp2(gap * (gap * scale))


def moments_kernel(group, count, fresh, *refs):
    if fresh:
        (
            atoms_ref, pos_ref, blocks_ref, widths_ref, pts_ref, phi_ref, dens_ref, w_ref,
            out_ref, wd_ref, dist_ref, polar_ref, side_ref, scale_ref,
        ) = refs
    else:
        (
            atoms_ref, pos_ref, blocks_ref, widths_ref, pts_ref, wd_ref,
            out_ref, dist_ref, polar_ref, side_ref, scale_ref,
        ) = refs
    points = pts_ref.shape[2]
    if fresh:
        for start in range(0, points, 256):
            here = pl.ds(start, 256)
            phi = phi_ref[0, :, here]
            wide = phi.astype(jnp.float32)
            for c in range(3):
                product = jnp.dot(dens_ref[0, c], phi, preferred_element_type=jnp.float32)
                density = jnp.sum(wide * product, axis=0, keepdims=True)
                wd_ref[pl.ds(c, 1), here] = w_ref[:, here] * density
    atom_at = atom_finder(group, atoms_ref)
    prepare([atom_at(i) for i in range(count)], pos_ref, pts_ref, dist_ref, polar_ref, side_ref)
    prepare_shells(widths_ref, scale_ref)

    def body(k, carry):
        blocks = blocks_ref[atom_at(k)]

        live = S
        middle, scale = shell_columns(blocks, live, scale_ref)
        total = jnp.zeros((3 * live, S), jnp.float32)
        for start in range(0, points, 256):
            scaled, angles = [[], [], []], []
            for inner in (start, start + LANES):
                t = inner // LANES
                radial = radial_tile(k, t, middle, scale, dist_ref).astype(jnp.bfloat16)
                angles.append(angular_tile(k, count, t, polar_ref, side_ref))
                for c in range(3):
                    row = jnp.broadcast_to(wd_ref[pl.ds(c, 1), pl.ds(inner, LANES)], (16, LANES))
                    row = jnp.concatenate([row.astype(jnp.bfloat16)] * (live // 16), axis=0)
                    scaled[c].append(radial * row)
            left = jnp.concatenate([jnp.concatenate(s, axis=1) for s in scaled], axis=0)
            right = jnp.concatenate(angles, axis=1)
            total += lax.dot_general(left, right, NT, preferred_element_type=jnp.float32)
        half = live // 2
        for c in range(3):
            even = total[c * live : c * live + half]
            odd = total[c * live + half : (c + 1) * live]
            block = jnp.concatenate([even, odd], axis=1)
            if live < S:
                rest = jnp.zeros((S // 2 - half, LANES), jnp.float32)
                block = jnp.concatenate([block, rest], axis=0)
            out_ref[k, pl.ds(c * (S // 2), S // 2), :] = block.astype(out_ref.dtype)

        return carry

    lax.fori_loop(0, count, body, 0, unroll=8)


def table_scratch(count, points):
    tiles = points // LANES
    return [
        pltpu.VMEM((tiles, count, LANES), jnp.float32),
        pltpu.VMEM((tiles, DEG * count, LANES), jnp.float32),
        pltpu.VMEM((tiles, DEG * count, LANES), jnp.float32),
        pltpu.VMEM((S, LANES), jnp.float32),
    ]


def table_cost(count, points):
    cells = count * points * S
    return pl.CostEstimate(flops=cells * 3 * S * 2, bytes_accessed=cells, transcendentals=cells)


def moments_call(group, count, shared, wd=None, phi=None, dens=None, w=None):
    points = shared[-1].shape[2]
    fresh = wd is None
    out = [jax.ShapeDtypeStruct((count, 3 * S // 2, LANES), jnp.bfloat16)]
    args = list(shared)
    if fresh:
        out.append(jax.ShapeDtypeStruct((3, points), jnp.float32))
        args += [phi, dens, w]
    else:
        args += [wd]
    return pl.pallas_call(
        functools.partial(moments_kernel, group, count, fresh),
        out_shape=out,
        in_specs=[SMEM] * 4 + [VMEM] * (len(args) - 4),
        out_specs=[VMEM] * len(out),
        scratch_shapes=table_scratch(count, points),
        cost_estimate=table_cost(count, points),
        compiler_params=pltpu.CompilerParams(vmem_limit_bytes=20 << 20),
        name="moments",
    )(*args)


def field_kernel(groups, size, carried, kept, last, tile, *refs):
    (atoms_ref, pos_ref, blocks_ref, widths_ref, pts_ref), refs = refs[:5], refs[5:]
    tabs, refs = refs[: len(groups)], refs[len(groups) :]
    count = len(groups) * size
    if carried:
        acc_in, refs = refs[0], refs[1:]
    if last:
        (phi_ref, w_ref, label_ref), outs, refs = refs[:3], refs[3:7], refs[7:]
    else:
        acc_ref, refs = refs[0], refs[1:]
    if kept:
        plane_ref, refs = refs[0], refs[1:]
    dist_ref, polar_ref, side_ref, scale_ref = refs[:4]
    if last:
        acc_ref, oper_ref, marks_ref = refs[4:7]
    points = pts_ref.shape[2]
    finders = [atom_finder(group, atoms_ref) for group in groups]
    prepare([atom_at(i) for atom_at in finders for i in range(size)], pos_ref, pts_ref, dist_ref, polar_ref, side_ref)
    prepare_shells(widths_ref, scale_ref)
    acc_ref[...] = acc_in[...] if carried else jnp.zeros_like(acc_ref)
    if kept:
        for order in range(len(groups)):
            plane_ref[order ^ lax.axis_index("col")] = tabs[order][lax.axis_index("batch")]

    def body(i, carry, order, atom_at):
        k = order * size + i
        blocks = blocks_ref[atom_at(i)]

        live, half = S, S // 2
        middle, scale = shell_columns(blocks, live, scale_ref)
        table = tabs[order][i].astype(jnp.float32)
        lines = []
        for c in range(3):
            block = table[c * (S // 2) : c * (S // 2) + half]
            lines += [block[:, :S], block[:, S:]]
        left = jnp.concatenate(lines, axis=0).astype(jnp.bfloat16)
        for start in range(0, points, 256):
            t = start // LANES
            right = jnp.concatenate(
                [angular_tile(k, count, t + d, polar_ref, side_ref) for d in range(2)], axis=1
            )
            spread = jnp.dot(left, right, preferred_element_type=jnp.float32)
            for d in range(2):
                here = pl.ds(start + d * LANES, LANES)
                radial = radial_tile(k, t + d, middle, scale, dist_ref)
                for c in range(3):
                    sums = acc_ref[pl.ds(8 * c, 8), here]
                    for r in range(0, live, 8):
                        at = c * live + r
                        sums += radial[r : r + 8] * spread[at : at + 8, d * LANES : (d + 1) * LANES]
                    acc_ref[pl.ds(8 * c, 8), here] = sums

        return carry

    for order, atom_at in enumerate(finders):
        step = functools.partial(body, order=order, atom_at=atom_at)
        lax.fori_loop(0, size, step, 0, unroll=4)
    if last:
        piece = phi_ref.shape[1] // 2
        third = piece // 3
        for h in range(2):
            strips = [label_ref[:, h * piece + b * third : h * piece + (b + 1) * third] for b in range(3)]
            inner = jnp.concatenate(strips, axis=0) - h * tile
            digits = [(inner >> 5).astype(jnp.float32), (inner & 31).astype(jnp.float32)]
            marks_ref[h] = jnp.concatenate(digits + [jnp.zeros((2, third), jnp.float32)], axis=0)
        sides = (lax.axis_index("row"), lax.axis_index("col"))
        halves = [[flip ^ side for flip in range(2)] for side in sides]
        spans = [[pl.ds(pl.multiple_of(h * piece, 32), piece) for h in pair] for pair in halves]
        quads = {}
        for c in range(3):
            for start in range(0, points, 256):
                here = pl.ds(start, 256)
                total = jnp.sum(acc_ref[pl.ds(8 * c, 8), here], axis=0, keepdims=True)
                wide = phi_ref[0, :, here].astype(jnp.float32)
                oper_ref[:, here] = (wide * (w_ref[:, here] * total)).astype(jnp.bfloat16)
            for x in range(2):
                for y in range(2):
                    quads[c, x, y] = lax.dot_general(
                        oper_ref[spans[0][x], :],
                        phi_ref[0, spans[1][y], :],
                        NT,
                        preferred_element_type=jnp.float32,
                    )
        for x in range(2):
            for y in range(2):
                q0, q1, q2 = (quads[c, x, y] for c in range(3))
                marks = [marks_ref[halves[0][x]], marks_ref[halves[1][y]]]
                marks = jnp.concatenate(marks + [jnp.zeros((third - 16, third), jnp.float32)], axis=0)
                parts = [q2[b * third : (b + 1) * third, 2 * third :] for b in range(3)] + [marks]
                blocks = [
                    jnp.concatenate([q0, q2[:, :third]], axis=1),
                    jnp.concatenate([q1, q2[:, third : 2 * third]], axis=1),
                    jnp.concatenate(parts, axis=1),
                ]
                outs[2 * y + x][0] = jnp.concatenate(blocks, axis=0).astype(jnp.bfloat16)


def field_call(groups, size, shared, tables, acc=None, keep=True, ends=None):
    points = shared[-1].shape[2]
    last = ends is not None
    count = len(groups) * size
    args = list(shared) + list(tables) + ([] if acc is None else [acc])
    scratch = table_scratch(count, points)
    if last:
        args += ends
        third = ends[0].shape[1] // 6
        out = [jax.ShapeDtypeStruct((1, 7 * third, LANES), jnp.bfloat16)] * 4
        scratch += [
            pltpu.VMEM((24, points), jnp.float32),
            pltpu.VMEM(ends[0].shape[1:], jnp.bfloat16),
            pltpu.VMEM((2, 8, third), jnp.float32),
        ]
    else:
        out = [jax.ShapeDtypeStruct((24, points), jnp.float32)]
    if keep:
        out.append(jax.ShapeDtypeStruct((len(groups),) + tables[0].shape[1:], jnp.bfloat16))
    return pl.pallas_call(
        functools.partial(field_kernel, groups, size, acc is not None, keep, last, NB // 2),
        out_shape=out,
        in_specs=[SMEM] * 4 + [VMEM] * (len(args) - 4),
        out_specs=[VMEM] * len(out),
        scratch_shapes=scratch,
        cost_estimate=table_cost(count, points),
        compiler_params=pltpu.CompilerParams(vmem_limit_bytes=20 << 20),
        name="field",
    )(*args)


def place_kernel(pieces, carried, final, piece, tile, *refs):
    stacks, refs = refs[:pieces], refs[pieces:]
    if carried:
        acc_in, refs = refs[0], refs[1:]
    out_ref, rows_ref, wide_ref = refs[:3]
    if final:
        hold_ref, sem_ref = refs[3:]
    third = piece // 3
    group = 4
    total = rows_ref.shape[1] // piece
    lane = lax.broadcasted_iota(jnp.int32, (piece, LANES), 1).astype(jnp.int16)
    sub = lax.broadcasted_iota(jnp.int32, (tile, LANES), 0).astype(jnp.int16)
    one, zero = jnp.bfloat16(1), jnp.bfloat16(0)
    per = total // pieces
    for first in range(0, total, group):
        strips = []
        for g in range(first, first + group):
            ref, at = stacks[g // per], g % per
            tail = ref[at, pl.ds(2 * piece, third), :].astype(jnp.float32)
            marks = tail[: third // 2, 3 * third :]
            row_mark = marks[0:3] * 32.0 + marks[3:6]
            col_mark = marks[8:11] * 32.0 + marks[11:14]
            strips += [row_mark[b : b + 1] for b in range(3)]
            flat = jnp.concatenate([col_mark[b : b + 1] for b in range(3)] + [col_mark[0:1]], axis=1)
            column = jnp.transpose(jnp.broadcast_to(flat, (LANES, LANES)))[:piece].astype(jnp.int32).astype(jnp.int16)
            hits = jnp.concatenate(
                [
                    jnp.where(column == lane + u, one, zero)
                    for u in range(0, tile, LANES)
                ],
                axis=1,
            )
            upper = ref[at, pl.ds(0, piece), :].astype(jnp.float32)
            lower = ref[at, pl.ds(piece, piece), :].astype(jnp.float32)
            rest = jnp.concatenate([tail[:, b * third : (b + 1) * third] for b in range(3)], axis=0)
            shared = jnp.concatenate([upper[:, piece:], lower[:, piece:], rest], axis=1)
            quads = jnp.concatenate([upper[:, :piece], lower[:, :piece], shared], axis=0)
            spread = jnp.dot(
                quads.astype(jnp.bfloat16), hits, preferred_element_type=jnp.float32
            ).astype(jnp.bfloat16)
            for c in range(3):
                wide_ref[c, pl.ds(g * piece, piece), :] = spread[c * piece : (c + 1) * piece]
        strip = jnp.concatenate(strips, axis=1).astype(jnp.int32)
        strip = jnp.broadcast_to(strip, (16, strip.shape[1])).astype(jnp.int16)
        strip = jnp.concatenate([strip] * (tile // 16), axis=0)
        for start in range(0, group * piece, LANES):
            rows_ref[:, pl.ds(first * piece + start, LANES)] = (
                jnp.where(sub == strip[:, start : start + LANES], one, zero)
            )

    copies = []
    for c in range(3):
        value = jnp.dot(rows_ref[...], wide_ref[c], preferred_element_type=jnp.float32)
        if carried:
            value += acc_in[c]
        if final:
            hold_ref[c] = value.astype(out_ref.dtype)
            copies.append(pltpu.make_async_copy(hold_ref.at[c], out_ref.at[c], sem_ref.at[c]))
            copies[-1].start()
        else:
            out_ref[c] = value
    for copy in copies:
        copy.wait()


def place_call(stacks, piece, tile, acc=None, final=True):
    total = sum(stack.shape[0] for stack in stacks)
    depth = total * piece
    args = list(stacks) + ([] if acc is None else [acc])
    return pl.pallas_call(
        functools.partial(place_kernel, len(stacks), acc is not None, final, piece, tile),
        out_shape=jax.ShapeDtypeStruct((3, tile, tile), jnp.bfloat16 if final else jnp.float32),
        in_specs=[VMEM] * len(args),
        out_specs=pl.BlockSpec(memory_space=pl.ANY) if final else VMEM,
        scratch_shapes=[
            pltpu.VMEM((tile, depth), jnp.bfloat16),
            pltpu.VMEM((3, depth, tile), jnp.bfloat16),
        ]
        + ([pltpu.VMEM((3, tile, tile), jnp.bfloat16), pltpu.SemaphoreType.DMA((3,))] if final else []),
        input_output_aliases={} if acc is None or final else {len(stacks): 0},
        compiler_params=pltpu.CompilerParams(vmem_limit_bytes=28 << 20),
        cost_estimate=pl.CostEstimate(
            flops=8 * 3 * depth * tile * tile, bytes_accessed=12 * tile * tile, transcendentals=0
        ),
        name="place",
    )(*args)


def apply_green(charges, kernels):
    shaped = charges.astype(jnp.bfloat16).reshape(-1, 3, S, DEG, DEG)
    kernel_rows = kernels.reshape(-1, DEG, S, S)
    result = jnp.einsum(
        "xast,xctam->xcsam", kernel_rows, shaped, preferred_element_type=jnp.float32
    )
    return result.astype(jnp.bfloat16).reshape(-1, 3 * S * DEG * DEG)


def swap(value, axis, mask=1):
    size = lax.axis_size(axis)
    return lax.ppermute(value, axis, [(i, i ^ mask) for i in range(size)])


def on_device(
    basis_values,
    density_matrix,
    points,
    weights,
    intersection,
    basis_index,
    atom_positions,
    shell_blocks,
    shell_widths,
    green,
):
    atoms = intersection[0]
    labels = basis_index[0]
    owners = lax.axis_size("batch")
    parts = lax.axis_size("row")
    sides = lax.axis_size("col")
    row, col = lax.axis_index("row"), lax.axis_index("col")
    count = atoms.shape[0]
    slots = (count + owners - 1) // owners
    holding = green.shape[0]
    every_atom = atom_positions.shape[1]
    width = 3 * S * DEG * DEG
    lines = width // LANES
    highest = lax.Precision.HIGHEST
    dense = count == every_atom and holding == parts * sides
    plane = ("row", "col")
    across = [(i, i ^ 3) for i in range(parts * sides)]
    half, group = count // 2, count // 4
    shared = (atoms, atom_positions, shell_blocks, shell_widths, jnp.swapaxes(points, 0, 1))
    wanted = ((sides, None, 0), (sides, None, 1)) if dense else (0, half)
    listed = [(holding, f & 1, f >> 1) if dense else f * group for f in range(4)]
    other, weighted = moments_call(
        wanted[1], half, shared, phi=basis_values, dens=density_matrix, w=weights
    )
    mate = swap(other, "col") if dense else other
    first = moments_call(wanted[0], half, shared, wd=weighted)[0]
    if dense:
        held = first + mate
        shares = lax.all_to_all(held, ("batch", "row"), split_axis=0, concat_axis=0, tiled=True)
        charges = jnp.sum(shares.astype(jnp.float32), axis=0)
        kernels = lax.dynamic_index_in_dim(green, row * sides + col, 0, keepdims=True)
        mine = apply_green(charges.reshape(1, width), kernels).reshape(1, lines, LANES)
        own = lax.all_to_all(
            jnp.broadcast_to(mine, (owners, lines, LANES)),
            "batch",
            split_axis=0,
            concat_axis=0,
            tiled=True,
        )
        beside = swap(own, "row")
        beyond = lax.ppermute(own, plane, across)
        tables = [own, beside, swap(own, "col"), beyond]
    else:
        moments = jnp.concatenate([first, other])
        moments = moments.astype(jnp.float32).reshape(count, width)
        home = atoms // holding
        local_slot = atoms % holding
        order = jnp.arange(count)
        before = (home[None, :] == home[:, None]) & (order[None, :] < order[:, None])
        place = home * slots + jnp.sum(before, axis=1)
        routing = jnp.arange(owners * slots)[:, None] == place[None, :]
        outgoing = jnp.dot(routing.astype(jnp.float32), moments, precision=highest).reshape(
            owners, slots, width
        )
        tags = (jnp.sum(jnp.where(routing, local_slot[None, :] + 1, 0), axis=1) - 1).reshape(
            owners, slots
        )
        incoming, sources = (
            lax.all_to_all(outgoing, "batch", split_axis=0, concat_axis=0, tiled=True),
            lax.all_to_all(tags, "batch", split_axis=0, concat_axis=0, tiled=True),
        )
        collect = jnp.arange(holding)[:, None] == sources.reshape(1, owners * slots)
        partial_value = jnp.dot(
            collect.astype(jnp.float32), incoming.reshape(owners * slots, width), precision=highest
        )
        totals = lax.psum(partial_value, ("row", "col"))
        potential = apply_green(totals, green)
        back = jnp.dot(
            collect.T.astype(jnp.bfloat16), potential, preferred_element_type=jnp.float32
        ).astype(jnp.bfloat16)
        returned = lax.all_to_all(
            back.reshape(owners, slots, width), "batch", split_axis=0, concat_axis=0, tiled=True
        )
        table = jnp.dot(
            routing.T.astype(jnp.bfloat16),
            returned.reshape(owners * slots, width),
            preferred_element_type=jnp.float32,
        )
        table = table.astype(jnp.bfloat16).reshape(count, lines, LANES)
        tables = [table[place * group : (place + 1) * group] for place in range(4)]
    piece = labels.shape[0] // parts
    tile = NB // parts
    ends = [basis_values, weights, basis_index]
    spread = functools.partial(field_call, size=group, shared=shared, keep=dense)
    field, *ours = spread((listed[0], listed[2]), tables=[tables[0], tables[2]])
    load = spread((listed[1], listed[3]), tables=[tables[1], tables[3]], acc=field, ends=ends)
    if dense:
        ours, theirs = ours[0], load[4]
        potential = jnp.concatenate(
            [jnp.where(row == 0, ours, theirs), jnp.where(row == 0, theirs, ours)]
        ).reshape(holding, width)
    got = [swap(load[2], "col"), swap(load[1], "row"), lax.ppermute(load[3], plane, across)]
    plane_load = jnp.concatenate([load[0]] + got, axis=0)
    if owners <= 8:
        near, far = [plane_load], []
        for step in range(2, owners, 2):
            near.append(swap(plane_load, "batch", step))
        for line in near:
            far.append(swap(line, "batch"))
        stages = [near[:1]] + [list(pair) for pair in zip(near[1:], far)] + [far[-1:]]
        total = None
        for order, lines in enumerate(stages):
            total = place_call(lines, piece, tile, total, final=lines is stages[-1])
        hamiltonian = total
    else:
        everyone = lax.all_gather(plane_load, "batch", axis=0)
        chunk = 2
        everyone = everyone.reshape((owners // chunk, chunk * 4) + plane_load.shape[1:])

        def add(total, item):
            return place_call([item], piece, tile, total, final=False), None

        total, _ = lax.scan(add, jnp.zeros((3, tile, tile), jnp.float32), everyone)
        hamiltonian = total.astype(jnp.bfloat16)
    return (potential, hamiltonian)


def solution(mesh):
    return jax.shard_map(
        on_device,
        mesh=mesh,
        in_specs=(
            P(("batch", "row", "col"), None, None),
            P(("batch", "row", "col"), None, None, None),
            P(("batch", "row", "col"), None, None),
            P(("batch", "row", "col"), None),
            P(("batch", "row", "col"), None),
            P(("batch", "row", "col"), None),
            P(),
            P(),
            P(),
            P("batch", None, None),
        ),
        out_specs=(P("batch", None), P(None, "row", "col")),
        check_vma=False,
    )
```

```python
import functools

import jax
import jax.numpy as jnp
from jax import lax
from jax.experimental import pallas as pl
from jax.experimental.pallas import tpu as pltpu
from jax.sharding import PartitionSpec as P


S = 64
DEG = 8
NB = 1536
LANES = 128
FAR = 1.0e6
LOG2E = 1.4426950408889634
NT = (((1,), (1,)), ((), ()))
SMEM = pl.BlockSpec(memory_space=pltpu.SMEM)
VMEM = pl.BlockSpec(memory_space=pltpu.VMEM)


def atom_finder(group, atoms_ref):
    if isinstance(group, int):
        return lambda i: atoms_ref[group + i]
    stride, row_flip, col_flip = group
    base = lax.axis_index("col") ^ col_flip
    if row_flip is not None:
        base = base + (lax.axis_index("row") ^ row_flip) * 2
    return lambda i: base + i * stride


def prepare(chosen, pos_ref, pts_ref, dist_ref, polar_ref, side_ref):
    count = len(chosen)
    rows = lax.broadcasted_iota(jnp.int32, (count, LANES), 0)
    centre = []
    for axis in range(3):
        column = jnp.zeros((count, LANES), jnp.float32)
        for k, atom in enumerate(chosen):
            column = jnp.where(rows == k, pos_ref[axis, atom], column)
        centre.append(column)
    for t in range(pts_ref.shape[2] // LANES):
        here = pl.ds(t * LANES, LANES)
        delta = [pts_ref[axis, :, here] - centre[axis] for axis in range(3)]
        square = delta[0] * delta[0] + delta[1] * delta[1] + delta[2] * delta[2] + 0.01
        inverse = lax.rsqrt(square)
        dist_ref[t] = square * inverse
        for ladder, u in ((polar_ref, delta[2] * inverse), (side_ref, delta[0] * inverse)):
            older, old = jnp.ones_like(u), u
            ladder[t, pl.ds(0, count), :] = older
            ladder[t, pl.ds(count, count), :] = old
            for order in range(2, DEG):
                older, old = old, 2.0 * u * old - older
                ladder[t, pl.ds(order * count, count), :] = old


def prepare_shells(widths_ref, scale_ref):
    rows = lax.broadcasted_iota(jnp.int32, (8, LANES), 0)
    for start in range(0, S, 8):
        column = jnp.zeros((8, LANES), jnp.float32)
        for j in range(8):
            place = start + j
            shell = 2 * place if place < S // 2 else 2 * place - (S - 1)
            column = jnp.where(rows == j, widths_ref[shell], column)
        scale_ref[pl.ds(start, 8), :] = -LOG2E / (column * column)


def shell_columns(blocks, live, scale_ref):
    half = live // 2
    place = lax.broadcasted_iota(jnp.int32, (live, LANES), 0)
    shell = jnp.where(place < half, 2 * place, 2 * place - (live - 1))
    middle = jnp.where(shell < 8 * blocks, shell.astype(jnp.float32) * (4.0 / S), FAR)
    scale = jnp.concatenate(
        [scale_ref[pl.ds(0, half), :], scale_ref[pl.ds(S // 2, half), :]], axis=0
    )
    return middle, scale


def angular_tile(k, count, t, polar_ref, side_ref):
    side = side_ref[t, pl.ds(k, DEG, stride=count), :]
    return jnp.concatenate(
        [
            polar_ref[t, pl.ds(order * count + k, DEG, stride=0), :] * side
            for order in range(DEG)
        ],
        axis=0,
    ).astype(jnp.bfloat16)


def radial_tile(k, t, middle, scale, dist_ref):
    dist = dist_ref[t, pl.ds(k, 8, stride=0), :]
    gap = jnp.concatenate([dist] * (middle.shape[0] // 8), axis=0) - middle
    return jnp.exp2(gap * (gap * scale))


def moments_kernel(group, count, fresh, *refs):
    if fresh:
        (
            atoms_ref, pos_ref, blocks_ref, widths_ref, pts_ref, phi_ref, dens_ref, w_ref,
            out_ref, wd_ref, dist_ref, polar_ref, side_ref, scale_ref,
        ) = refs
    else:
        (
            atoms_ref, pos_ref, blocks_ref, widths_ref, pts_ref, wd_ref,
            out_ref, dist_ref, polar_ref, side_ref, scale_ref,
        ) = refs
    points = pts_ref.shape[2]
    if fresh:
        for start in range(0, points, 256):
            here = pl.ds(start, 256)
            phi = phi_ref[0, :, here]
            wide = phi.astype(jnp.float32)
            for c in range(3):
                product = jnp.dot(dens_ref[0, c], phi, preferred_element_type=jnp.float32)
                density = jnp.sum(wide * product, axis=0, keepdims=True)
                wd_ref[pl.ds(c, 1), here] = w_ref[:, here] * density
    atom_at = atom_finder(group, atoms_ref)
    prepare([atom_at(i) for i in range(count)], pos_ref, pts_ref, dist_ref, polar_ref, side_ref)
    prepare_shells(widths_ref, scale_ref)

    def body(k, carry):
        blocks = blocks_ref[atom_at(k)]

        live = S
        middle, scale = shell_columns(blocks, live, scale_ref)
        total = jnp.zeros((3 * live, S), jnp.float32)
        for start in range(0, points, 256):
            scaled, angles = [[], [], []], []
            for inner in (start, start + LANES):
                t = inner // LANES
                radial = radial_tile(k, t, middle, scale, dist_ref).astype(jnp.bfloat16)
                angles.append(angular_tile(k, count, t, polar_ref, side_ref))
                for c in range(3):
                    row = jnp.broadcast_to(wd_ref[pl.ds(c, 1), pl.ds(inner, LANES)], (16, LANES))
                    row = jnp.concatenate([row.astype(jnp.bfloat16)] * (live // 16), axis=0)
                    scaled[c].append(radial * row)
            left = jnp.concatenate([jnp.concatenate(s, axis=1) for s in scaled], axis=0)
            right = jnp.concatenate(angles, axis=1)
            total += lax.dot_general(left, right, NT, preferred_element_type=jnp.float32)
        half = live // 2
        for c in range(3):
            even = total[c * live : c * live + half]
            odd = total[c * live + half : (c + 1) * live]
            block = jnp.concatenate([even, odd], axis=1)
            if live < S:
                rest = jnp.zeros((S // 2 - half, LANES), jnp.float32)
                block = jnp.concatenate([block, rest], axis=0)
            out_ref[k, pl.ds(c * (S // 2), S // 2), :] = block.astype(out_ref.dtype)

        return carry

    lax.fori_loop(0, count, body, 0, unroll=8)


def table_scratch(count, points):
    tiles = points // LANES
    return [
        pltpu.VMEM((tiles, count, LANES), jnp.float32),
        pltpu.VMEM((tiles, DEG * count, LANES), jnp.float32),
        pltpu.VMEM((tiles, DEG * count, LANES), jnp.float32),
        pltpu.VMEM((S, LANES), jnp.float32),
    ]


def table_cost(count, points):
    cells = count * points * S
    return pl.CostEstimate(flops=cells * 3 * S * 2, bytes_accessed=cells, transcendentals=cells)


def moments_call(group, count, shared, wd=None, phi=None, dens=None, w=None):
    points = shared[-1].shape[2]
    fresh = wd is None
    out = [jax.ShapeDtypeStruct((count, 3 * S // 2, LANES), jnp.bfloat16)]
    args = list(shared)
    if fresh:
        out.append(jax.ShapeDtypeStruct((3, points), jnp.float32))
        args += [phi, dens, w]
    else:
        args += [wd]
    return pl.pallas_call(
        functools.partial(moments_kernel, group, count, fresh),
        out_shape=out,
        in_specs=[SMEM] * 4 + [VMEM] * (len(args) - 4),
        out_specs=[VMEM] * len(out),
        scratch_shapes=table_scratch(count, points),
        cost_estimate=table_cost(count, points),
        name="moments",
    )(*args)


def field_kernel(groups, size, carried, kept, last, tile, *refs):
    (atoms_ref, pos_ref, blocks_ref, widths_ref, pts_ref), refs = refs[:5], refs[5:]
    tabs, refs = refs[: len(groups)], refs[len(groups) :]
    count = len(groups) * size
    if carried:
        acc_in, refs = refs[0], refs[1:]
    if last:
        (phi_ref, w_ref, label_ref), outs, refs = refs[:3], refs[3:7], refs[7:]
    else:
        acc_ref, refs = refs[0], refs[1:]
    if kept:
        plane_ref, refs = refs[0], refs[1:]
    dist_ref, polar_ref, side_ref, scale_ref = refs[:4]
    if last:
        acc_ref, oper_ref, marks_ref = refs[4:7]
    points = pts_ref.shape[2]
    finders = [atom_finder(group, atoms_ref) for group in groups]
    prepare([atom_at(i) for atom_at in finders for i in range(size)], pos_ref, pts_ref, dist_ref, polar_ref, side_ref)
    prepare_shells(widths_ref, scale_ref)
    acc_ref[...] = acc_in[...] if carried else jnp.zeros_like(acc_ref)
    if kept:
        for order in range(len(groups)):
            at = order ^ lax.axis_index("col") if len(groups) == 2 else order
            plane_ref[at] = tabs[order][lax.axis_index("batch")]

    def body(i, carry, order, atom_at):
        k = order * size + i
        blocks = blocks_ref[atom_at(i)]

        live, half = S, S // 2
        middle, scale = shell_columns(blocks, live, scale_ref)
        table = tabs[order][i].astype(jnp.float32)
        lines = []
        for c in range(3):
            block = table[c * (S // 2) : c * (S // 2) + half]
            lines += [block[:, :S], block[:, S:]]
        left = jnp.concatenate(lines, axis=0).astype(jnp.bfloat16)
        for start in range(0, points, 256):
            t = start // LANES
            right = jnp.concatenate(
                [angular_tile(k, count, t + d, polar_ref, side_ref) for d in range(2)], axis=1
            )
            spread = jnp.dot(left, right, preferred_element_type=jnp.float32)
            for d in range(2):
                here = pl.ds(start + d * LANES, LANES)
                radial = radial_tile(k, t + d, middle, scale, dist_ref)
                for c in range(3):
                    sums = acc_ref[pl.ds(8 * c, 8), here]
                    for r in range(0, live, 8):
                        at = c * live + r
                        sums += radial[r : r + 8] * spread[at : at + 8, d * LANES : (d + 1) * LANES]
                    acc_ref[pl.ds(8 * c, 8), here] = sums

        return carry

    for order, atom_at in enumerate(finders):
        step = functools.partial(body, order=order, atom_at=atom_at)
        lax.fori_loop(0, size, step, 0, unroll=4)
    if last:
        piece = phi_ref.shape[1] // 2
        third = piece // 3
        for h in range(2):
            strips = [label_ref[:, h * piece + b * third : h * piece + (b + 1) * third] for b in range(3)]
            inner = jnp.concatenate(strips, axis=0) - h * tile
            digits = [(inner >> 5).astype(jnp.float32), (inner & 31).astype(jnp.float32)]
            marks_ref[h] = jnp.concatenate(digits + [jnp.zeros((2, third), jnp.float32)], axis=0)
        sides = (lax.axis_index("row"), lax.axis_index("col"))
        halves = [[flip ^ side for flip in range(2)] for side in sides]
        spans = [[pl.ds(pl.multiple_of(h * piece, 32), piece) for h in pair] for pair in halves]
        quads = {}
        for c in range(3):
            for start in range(0, points, 256):
                here = pl.ds(start, 256)
                total = jnp.sum(acc_ref[pl.ds(8 * c, 8), here], axis=0, keepdims=True)
                wide = phi_ref[0, :, here].astype(jnp.float32)
                oper_ref[:, here] = (wide * (w_ref[:, here] * total)).astype(jnp.bfloat16)
            for x in range(2):
                for y in range(2):
                    quads[c, x, y] = lax.dot_general(
                        oper_ref[spans[0][x], :],
                        phi_ref[0, spans[1][y], :],
                        NT,
                        preferred_element_type=jnp.float32,
                    )
        for x in range(2):
            for y in range(2):
                q0, q1, q2 = (quads[c, x, y] for c in range(3))
                marks = [marks_ref[halves[0][x]], marks_ref[halves[1][y]]]
                marks = jnp.concatenate(marks + [jnp.zeros((third - 16, third), jnp.float32)], axis=0)
                parts = [q2[b * third : (b + 1) * third, 2 * third :] for b in range(3)] + [marks]
                blocks = [
                    jnp.concatenate([q0, q2[:, :third]], axis=1),
                    jnp.concatenate([q1, q2[:, third : 2 * third]], axis=1),
                    jnp.concatenate(parts, axis=1),
                ]
                outs[2 * y + x][0] = jnp.concatenate(blocks, axis=0).astype(jnp.bfloat16)


def field_call(groups, size, shared, tables, acc=None, keep=True, ends=None):
    points = shared[-1].shape[2]
    last = ends is not None
    count = len(groups) * size
    args = list(shared) + list(tables) + ([] if acc is None else [acc])
    scratch = table_scratch(count, points)
    if last:
        args += ends
        third = ends[0].shape[1] // 6
        out = [jax.ShapeDtypeStruct((1, 7 * third, LANES), jnp.bfloat16)] * 4
        scratch += [
            pltpu.VMEM((24, points), jnp.float32),
            pltpu.VMEM(ends[0].shape[1:], jnp.bfloat16),
            pltpu.VMEM((2, 8, third), jnp.float32),
        ]
    else:
        out = [jax.ShapeDtypeStruct((24, points), jnp.float32)]
    if keep:
        out.append(jax.ShapeDtypeStruct((len(groups),) + tables[0].shape[1:], jnp.bfloat16))
    return pl.pallas_call(
        functools.partial(field_kernel, groups, size, acc is not None, keep, last, NB // 2),
        out_shape=out,
        in_specs=[SMEM] * 4 + [VMEM] * (len(args) - 4),
        out_specs=[VMEM] * len(out),
        scratch_shapes=scratch,
        cost_estimate=table_cost(count, points),
        compiler_params=pltpu.CompilerParams(vmem_limit_bytes=20 << 20),
        name="field",
    )(*args)


def place_kernel(pieces, carried, final, piece, tile, *refs):
    stacks, refs = refs[:pieces], refs[pieces:]
    if carried:
        acc_in, refs = refs[0], refs[1:]
    out_ref, rows_ref, wide_ref = refs[:3]
    if final:
        hold_ref, sem_ref = refs[3:]
    third = piece // 3
    group = 4
    total = rows_ref.shape[1] // piece
    lane = lax.broadcasted_iota(jnp.int32, (piece, LANES), 1).astype(jnp.int16)
    sub = lax.broadcasted_iota(jnp.int32, (tile, LANES), 0).astype(jnp.int16)
    one, zero = jnp.bfloat16(1), jnp.bfloat16(0)
    per = total // pieces
    for first in range(0, total, group):
        strips = []
        for g in range(first, first + group):
            ref, at = stacks[g // per], g % per
            tail = ref[at, pl.ds(2 * piece, third), :].astype(jnp.float32)
            marks = tail[: third // 2, 3 * third :]
            row_mark = marks[0:3] * 32.0 + marks[3:6]
            col_mark = marks[8:11] * 32.0 + marks[11:14]
            strips += [row_mark[b : b + 1] for b in range(3)]
            flat = jnp.concatenate([col_mark[b : b + 1] for b in range(3)] + [col_mark[0:1]], axis=1)
            column = jnp.transpose(jnp.broadcast_to(flat, (LANES, LANES)))[:piece].astype(jnp.int32).astype(jnp.int16)
            hits = jnp.concatenate(
                [
                    jnp.where(column == lane + u, one, zero)
                    for u in range(0, tile, LANES)
                ],
                axis=1,
            )
            upper = ref[at, pl.ds(0, piece), :].astype(jnp.float32)
            lower = ref[at, pl.ds(piece, piece), :].astype(jnp.float32)
            rest = jnp.concatenate([tail[:, b * third : (b + 1) * third] for b in range(3)], axis=0)
            shared = jnp.concatenate([upper[:, piece:], lower[:, piece:], rest], axis=1)
            quads = jnp.concatenate([upper[:, :piece], lower[:, :piece], shared], axis=0)
            spread = jnp.dot(
                quads.astype(jnp.bfloat16), hits, preferred_element_type=jnp.float32
            ).astype(jnp.bfloat16)
            for c in range(3):
                wide_ref[c, pl.ds(g * piece, piece), :] = spread[c * piece : (c + 1) * piece]
        strip = jnp.concatenate(strips, axis=1).astype(jnp.int32)
        strip = jnp.broadcast_to(strip, (16, strip.shape[1])).astype(jnp.int16)
        strip = jnp.concatenate([strip] * (tile // 16), axis=0)
        for start in range(0, group * piece, LANES):
            rows_ref[:, pl.ds(first * piece + start, LANES)] = (
                jnp.where(sub == strip[:, start : start + LANES], one, zero)
            )

    copies = []
    for c in range(3):
        value = jnp.dot(rows_ref[...], wide_ref[c], preferred_element_type=jnp.float32)
        if carried:
            value += acc_in[c]
        if final:
            hold_ref[c] = value.astype(out_ref.dtype)
            copies.append(pltpu.make_async_copy(hold_ref.at[c], out_ref.at[c], sem_ref.at[c]))
            copies[-1].start()
        else:
            out_ref[c] = value
    for copy in copies:
        copy.wait()


def place_call(stacks, piece, tile, acc=None, final=True):
    total = sum(stack.shape[0] for stack in stacks)
    depth = total * piece
    args = list(stacks) + ([] if acc is None else [acc])
    return pl.pallas_call(
        functools.partial(place_kernel, len(stacks), acc is not None, final, piece, tile),
        out_shape=jax.ShapeDtypeStruct((3, tile, tile), jnp.bfloat16 if final else jnp.float32),
        in_specs=[VMEM] * len(args),
        out_specs=pl.BlockSpec(memory_space=pl.ANY) if final else VMEM,
        scratch_shapes=[
            pltpu.VMEM((tile, depth), jnp.bfloat16),
            pltpu.VMEM((3, depth, tile), jnp.bfloat16),
        ]
        + ([pltpu.VMEM((3, tile, tile), jnp.bfloat16), pltpu.SemaphoreType.DMA((3,))] if final else []),
        input_output_aliases={} if acc is None or final else {len(stacks): 0},
        compiler_params=pltpu.CompilerParams(vmem_limit_bytes=28 << 20),
        cost_estimate=pl.CostEstimate(
            flops=8 * 3 * depth * tile * tile, bytes_accessed=12 * tile * tile, transcendentals=0
        ),
        name="place",
    )(*args)


def apply_green(charges, kernels):
    shaped = charges.astype(jnp.bfloat16).reshape(-1, 3, S, DEG, DEG)
    kernel_rows = kernels.reshape(-1, DEG, S, S)
    result = jnp.einsum(
        "xast,xctam->xcsam", kernel_rows, shaped, preferred_element_type=jnp.float32
    )
    return result.astype(jnp.bfloat16).reshape(-1, 3 * S * DEG * DEG)


def swap(value, axis, mask=1):
    size = lax.axis_size(axis)
    return lax.ppermute(value, axis, [(i, i ^ mask) for i in range(size)])


def on_device(
    basis_values,
    density_matrix,
    points,
    weights,
    intersection,
    basis_index,
    atom_positions,
    shell_blocks,
    shell_widths,
    green,
):
    atoms = intersection[0]
    labels = basis_index[0]
    owners = lax.axis_size("batch")
    parts = lax.axis_size("row")
    sides = lax.axis_size("col")
    row, col = lax.axis_index("row"), lax.axis_index("col")
    count = atoms.shape[0]
    slots = (count + owners - 1) // owners
    holding = green.shape[0]
    every_atom = atom_positions.shape[1]
    width = 3 * S * DEG * DEG
    lines = width // LANES
    highest = lax.Precision.HIGHEST
    dense = count == every_atom and holding == parts * sides
    plane = ("row", "col")
    across = [(i, i ^ 3) for i in range(parts * sides)]
    group = count // 4
    shared = (atoms, atom_positions, shell_blocks, shell_widths, jnp.swapaxes(points, 0, 1))
    listed = [(holding, f & 1, f >> 1) if dense else f * group for f in range(4)]
    third, weighted = moments_call(
        listed[3], group, shared, phi=basis_values, dens=density_matrix, w=weights
    )
    pieces = [None, None, None, third]
    if dense:
        mate = swap(third, "col")
    for f in (1, 2, 0):
        pieces[f] = moments_call(listed[f], group, shared, wd=weighted)[0]
    if dense:
        from_row = swap(pieces[1] + mate, "row")
        mate = swap(pieces[2], "col")
        held = (
            pieces[0].astype(jnp.float32)
            + mate.astype(jnp.float32)
            + from_row.astype(jnp.float32)
        ).astype(jnp.bfloat16)
        shares = lax.all_to_all(held, "batch", split_axis=0, concat_axis=0, tiled=True)
        charges = jnp.sum(shares.astype(jnp.float32), axis=0)
        kernels = lax.dynamic_index_in_dim(green, row * sides + col, 0, keepdims=True)
        mine = apply_green(charges.reshape(1, width), kernels).reshape(1, lines, LANES)
        own = lax.all_to_all(
            jnp.broadcast_to(mine, (owners, lines, LANES)),
            "batch",
            split_axis=0,
            concat_axis=0,
            tiled=True,
        )
        beside = swap(own, "row")
        beyond = swap(beside, "col")
        tables = [own, beside, swap(own, "col"), beyond]
    else:
        moments = jnp.concatenate(pieces)
        moments = moments.astype(jnp.float32).reshape(count, width)
        home = atoms // holding
        local_slot = atoms % holding
        order = jnp.arange(count)
        before = (home[None, :] == home[:, None]) & (order[None, :] < order[:, None])
        place = home * slots + jnp.sum(before, axis=1)
        routing = jnp.arange(owners * slots)[:, None] == place[None, :]
        outgoing = jnp.dot(routing.astype(jnp.float32), moments, precision=highest).reshape(
            owners, slots, width
        )
        tags = (jnp.sum(jnp.where(routing, local_slot[None, :] + 1, 0), axis=1) - 1).reshape(
            owners, slots
        )
        incoming, sources = (
            lax.all_to_all(outgoing, "batch", split_axis=0, concat_axis=0, tiled=True),
            lax.all_to_all(tags, "batch", split_axis=0, concat_axis=0, tiled=True),
        )
        collect = jnp.arange(holding)[:, None] == sources.reshape(1, owners * slots)
        partial_value = jnp.dot(
            collect.astype(jnp.float32), incoming.reshape(owners * slots, width), precision=highest
        )
        totals = lax.psum(partial_value, ("row", "col"))
        potential = apply_green(totals, green)
        back = jnp.dot(
            collect.T.astype(jnp.bfloat16), potential, preferred_element_type=jnp.float32
        ).astype(jnp.bfloat16)
        returned = lax.all_to_all(
            back.reshape(owners, slots, width), "batch", split_axis=0, concat_axis=0, tiled=True
        )
        table = jnp.dot(
            routing.T.astype(jnp.bfloat16),
            returned.reshape(owners * slots, width),
            preferred_element_type=jnp.float32,
        )
        table = table.astype(jnp.bfloat16).reshape(count, lines, LANES)
        tables = [table[place * group : (place + 1) * group] for place in range(4)]
    piece = labels.shape[0] // parts
    tile = NB // parts
    ends = [basis_values, weights, basis_index]
    spread = functools.partial(field_call, size=group, shared=shared, keep=dense)
    field, *ours = spread((listed[0], listed[2]), tables=[tables[0], tables[2]])
    field, *half = spread((listed[1],), tables=[tables[1]], acc=field)
    load = spread((listed[3],), tables=[tables[3]], acc=field, ends=ends)
    if dense:
        ours = ours[0]
        theirs = jnp.where(
            col == 0,
            jnp.concatenate([half[0], load[4]]),
            jnp.concatenate([load[4], half[0]]),
        )
        potential = jnp.concatenate(
            [jnp.where(row == 0, ours, theirs), jnp.where(row == 0, theirs, ours)]
        ).reshape(holding, width)
    got = [swap(load[2], "col"), swap(load[1], "row"), lax.ppermute(load[3], plane, across)]
    plane_load = jnp.concatenate([load[0]] + got, axis=0)
    if owners <= 8:
        near, far = [plane_load], []
        for step in range(2, owners, 2):
            near.append(swap(plane_load, "batch", step))
        for line in near:
            far.append(swap(line, "batch"))
        stages = [near[:1], far[:1]] + [near[1:2]] * (len(near) > 1)
        stages += [list(pair) for pair in zip(near[2:], far[1:])] + [far[-1:]] * (len(near) > 1)
        total = None
        for order, lines in enumerate(stages):
            total = place_call(lines, piece, tile, total, final=lines is stages[-1])
        hamiltonian = total
    else:
        everyone = lax.all_gather(plane_load, "batch", axis=0)
        chunk = 2
        everyone = everyone.reshape((owners // chunk, chunk * 4) + plane_load.shape[1:])

        def add(total, item):
            return place_call([item], piece, tile, total, final=False), None

        total, _ = lax.scan(add, jnp.zeros((3, tile, tile), jnp.float32), everyone)
        hamiltonian = total.astype(jnp.bfloat16)
    return (potential, hamiltonian)


def solution(mesh):
    return jax.shard_map(
        on_device,
        mesh=mesh,
        in_specs=(
            P(("batch", "row", "col"), None, None),
            P(("batch", "row", "col"), None, None, None),
            P(("batch", "row", "col"), None, None),
            P(("batch", "row", "col"), None),
            P(("batch", "row", "col"), None),
            P(("batch", "row", "col"), None),
            P(),
            P(),
            P(),
            P("batch", None, None),
        ),
        out_specs=(P("batch", None), P(None, "row", "col")),
        check_vma=False,
    )
```
